32 devices in a mesh: dp: 8 (over y, x, core), mp: 4 (over z).
Axes of the slice: x: 2, y: 2, z: 4, core: 2. Of those that a mesh axis runs over, the one named last changes fastest.
Arguments:
- latents: bfloat16 [32, 256, 16], P('dp'), may hold values from -6 to 6
- noise: bfloat16 [32, 256, 16], P('dp'), may hold values from -6 to 6
- labels: int32 [32], P('dp'), may hold values from 0 to 999
- time_index: int32 [32], P('dp'), may hold values from 0 to 999
- tables: float32 [1288, 768], P(None, 'dp'), may hold values from -2 to 2
- time_proj: float32 [768, 768], P('dp'), may hold values from -0.21875 to 0.21875
- modulation: float32 [768, 10752], P('dp', 'mp'), may hold values from -0.6 to 0.6
- qkv_proj: float32 [2, 768, 3, 768], P(None, 'dp', None, 'mp'), may hold values from -0.21875 to 0.21875
- out_proj: float32 [2, 768, 768], P(None, 'mp', 'dp'), may hold values from -0.875 to 0.875
- up_proj: float32 [2, 768, 3072], P(None, 'dp', 'mp'), may hold values from -0.21875 to 0.21875
- down_proj: float32 [2, 3072, 768], P(None, 'mp', 'dp'), may hold values from -0.109375 to 0.109375
- qkv_momentum: float32 [2, 768, 3, 768], P(None, 'dp', None, 'mp'), may hold values from -8.166273e-07 to 8.166273e-07
- out_momentum: float32 [2, 768, 768], P(None, 'mp', 'dp'), may hold values from -8.166273e-07 to 8.166273e-07
- up_momentum: float32 [2, 768, 3072], P(None, 'dp', 'mp'), may hold values from -8.166273e-07 to 8.166273e-07
- down_momentum: float32 [2, 3072, 768], P(None, 'mp', 'dp'), may hold values from -8.166273e-07 to 8.166273e-07
- tables_first: float32 [1288, 768], P(None, 'dp'), may hold values from -8.166273e-07 to 8.166273e-07
- tables_second: float32 [1288, 768], P(None, 'dp'), may hold values from 2.1923682e-15 to 8.7528006e-15
- time_first: float32 [768, 768], P('dp'), may hold values from -8.166273e-07 to 8.166273e-07
- time_second: float32 [768, 768], P('dp'), may hold values from 2.1923682e-15 to 8.7528006e-15
- mod_first: float32 [768, 10752], P('dp', 'mp'), may hold values from -8.166273e-07 to 8.166273e-07
- mod_second: float32 [768, 10752], P('dp', 'mp'), may hold values from 2.1923682e-15 to 8.7528006e-15
- adam_step: int32 [1], replicated, may hold values from 2 to 20
Outputs:
- loss: float32 [], replicated
- grad_norm: float32 [], replicated
- qkv_updated: float32 [2, 768, 3, 768], P(None, 'dp', None, 'mp')
- qkv_momentum_new: float32 [2, 768, 3, 768], P(None, 'dp', None, 'mp')
- out_updated: float32 [2, 768, 768], P(None, 'mp', 'dp')
- out_momentum_new: float32 [2, 768, 768], P(None, 'mp', 'dp')
- up_updated: float32 [2, 768, 3072], P(None, 'dp', 'mp')
- up_momentum_new: float32 [2, 768, 3072], P(None, 'dp', 'mp')
- down_updated: float32 [2, 3072, 768], P(None, 'mp', 'dp')
- down_momentum_new: float32 [2, 3072, 768], P(None, 'mp', 'dp')
- tables_updated: float32 [1288, 768], P(None, 'dp')
- tables_first_new: float32 [1288, 768], P(None, 'dp')
- tables_second_new: float32 [1288, 768], P(None, 'dp')
- time_updated: float32 [768, 768], P('dp')
- time_first_new: float32 [768, 768], P('dp')
- time_second_new: float32 [768, 768], P('dp')
- mod_updated: float32 [768, 10752], P('dp', 'mp')
- mod_first_new: float32 [768, 10752], P('dp', 'mp')
- mod_second_new: float32 [768, 10752], P('dp', 'mp')
The draws below stay inside these ranges and needn't reach their ends.
All inputs are finite; a program needn't handle non-finite values.
Results may differ from the reference program's by a relative error of at most 0.014.
The reference program's roundings to bfloat16 on the way count: a program that leaves them out, or rounds other values in their place, can miss the bound.
Values may be sent and summed in bfloat16 or wider, within the bound.
No kernel may reach another device: no remote copies, remote signals or barrier semaphores. Data moves between devices by JAX's collectives and lax.ppermute only.
A program may use at most 192 MiB of HBM per device.

```python
import math
import jax
import jax.numpy as jnp
from jax import lax

D = 768
HEADS = 12
FF = 3072
PATCH_IN = 16
FREQ = 256
CLASSES = 1000
GRID = 16
LAYERS = 2
MICRO = 2
NS_ITERS = 5
TSTEPS = 1000
SEQ_MB = 2
HD = 64
TOK = 256
SEQS = 32
ROWS_TAB = 1288
MODW = 10752
PARAMS = 23992320


def draw_tables(key, part):
    base = jnp.clip(jax.random.normal(key, (ROWS_TAB, D), jnp.float32), -4.0, 4.0)
    positions = jnp.arange(ROWS_TAB)[:, None]
    row_scale = jnp.where(positions < PATCH_IN, 0.25, jnp.where(positions < PATCH_IN + FREQ, FREQ ** (-0.5), jnp.where(positions < PATCH_IN + FREQ + CLASSES, 0.5, 0.05)))
    return base * row_scale


def with_ends(array, own_key, least, largest):
    place = [jax.random.randint(jax.random.fold_in(own_key, axis), (), 0, length) for axis, length in enumerate(array.shape)]
    widest = array.shape.index(max(array.shape))
    neighbour = place[:widest] + [(place[widest] + 1) % array.shape[widest]] + place[widest + 1:]
    return array.at[tuple(place)].set(least).at[tuple(neighbour)].set(largest)


def steps_of(rng, extent, cuts, low, top_value):
    level, own = 1.0, jax.random.fold_in(rng, 6)
    for dim, blocks in cuts:
        steps = jnp.exp(jax.random.uniform(jax.random.fold_in(own, dim), (blocks,), jnp.float32, low / len(cuts), top_value / len(cuts)))
        level = level * jnp.repeat(steps, extent[dim] // blocks).reshape([-1 if axis == dim else 1 for axis in range(len(extent))])
    return level


def bell_draw(key, extent, deviation, reach, shards=(), kind=jnp.bfloat16):
    entries = jax.random.normal(key, extent, jnp.float32) * deviation
    if len(shards) > 0:
        entries = steps_of(key, extent, shards, -0.22, 0.18) * entries
    return jnp.clip(entries, min=-reach, max=reach).astype(kind)


def setup_inputs(seed: int = 0) -> dict:
    arg_keys = jax.random.split(jax.random.key(seed), 23)
    latents = bell_draw(arg_keys[0], (SEQS, TOK, PATCH_IN), 1.0, 6.0, ((0, 8),))
    noise = bell_draw(arg_keys[1], (SEQS, TOK, PATCH_IN), 1.0, 6.0, ((0, 8),))
    labels = with_ends(jax.random.randint(arg_keys[2], (SEQS,), 0, CLASSES), jax.random.fold_in(arg_keys[2], 1), 0, CLASSES - 1).astype(jnp.int32)
    time_index = with_ends(jax.random.randint(arg_keys[3], (SEQS,), 0, TSTEPS), jax.random.fold_in(arg_keys[3], 1), 0, TSTEPS - 1).astype(jnp.int32)
    tables = draw_tables(jax.random.fold_in(arg_keys[22], 71), 0)
    time_proj = bell_draw(arg_keys[5], (D, D), D ** -0.5, 0.21875, ((0, 8),), jnp.float32)
    modulation = bell_draw(arg_keys[6], (D, MODW), 0.1, 0.6, ((0, 8), (1, 4)), jnp.float32)
    qkv_proj = bell_draw(arg_keys[7], (LAYERS, D, 3, D), D ** -0.5, 0.21875, ((1, 8), (3, 4)), jnp.float32)
    out_proj = bell_draw(arg_keys[8], (LAYERS, D, D), (D // 16) ** -0.5, 0.875, ((1, 4), (2, 8)), jnp.float32)
    up_proj = bell_draw(arg_keys[9], (LAYERS, D, FF), D ** -0.5, 0.21875, ((1, 8), (2, 4)), jnp.float32)
    down_proj = bell_draw(arg_keys[10], (LAYERS, FF, D), FF ** -0.5, 0.109375, ((1, 4), (2, 8)), jnp.float32)
    qkv_momentum = bell_draw(arg_keys[11], (LAYERS, D, 3, D), (0.001 / PARAMS ** 0.5), 8.166272777998529e-07, ((1, 8), (3, 4)), jnp.float32)
    out_momentum = bell_draw(arg_keys[12], (LAYERS, D, D), (0.001 / PARAMS ** 0.5), 8.166272777998529e-07, ((1, 4), (2, 8)), jnp.float32)
    up_momentum = bell_draw(arg_keys[13], (LAYERS, D, FF), (0.001 / PARAMS ** 0.5), 8.166272777998529e-07, ((1, 8), (2, 4)), jnp.float32)
    down_momentum = bell_draw(arg_keys[14], (LAYERS, FF, D), (0.001 / PARAMS ** 0.5), 8.166272777998529e-07, ((1, 4), (2, 8)), jnp.float32)
    tables_first = bell_draw(arg_keys[15], (ROWS_TAB, D), (0.001 / PARAMS ** 0.5), 8.166272777998529e-07, ((1, 8),), jnp.float32)
    tables_second = jnp.clip(jnp.exp(math.log(8.75280056089221e-15) - 1.3843914 * jax.random.uniform(arg_keys[16], (ROWS_TAB, D), jnp.float32) ** steps_of(arg_keys[16], (ROWS_TAB, D), ((1, 8),), -0.2, 0.2)), 2.192368177598254e-15, 8.75280056089221e-15)
    time_first = bell_draw(arg_keys[17], (D, D), (0.001 / PARAMS ** 0.5), 8.166272777998529e-07, ((0, 8),), jnp.float32)
    time_second = jnp.clip(jnp.exp(math.log(8.75280056089221e-15) - 1.3843914 * jax.random.uniform(arg_keys[18], (D, D), jnp.float32) ** steps_of(arg_keys[18], (D, D), ((0, 8),), -0.2, 0.2)), 2.192368177598254e-15, 8.75280056089221e-15)
    mod_first = bell_draw(arg_keys[19], (D, MODW), (0.001 / PARAMS ** 0.5), 8.166272777998529e-07, ((0, 8), (1, 4)), jnp.float32)
    mod_second = jnp.clip(jnp.exp(math.log(8.75280056089221e-15) - 1.3843914 * jax.random.uniform(arg_keys[20], (D, MODW), jnp.float32) ** steps_of(arg_keys[20], (D, MODW), ((0, 8), (1, 4)), -0.2, 0.2)), 2.192368177598254e-15, 8.75280056089221e-15)
    adam_step = jax.random.randint(arg_keys[21], (1,), 2, 21).astype(jnp.int32)
    return dict(latents=latents, noise=noise, labels=labels, time_index=time_index, tables=tables, time_proj=time_proj, modulation=modulation, qkv_proj=qkv_proj, out_proj=out_proj, up_proj=up_proj, down_proj=down_proj, qkv_momentum=qkv_momentum, out_momentum=out_momentum, up_momentum=up_momentum, down_momentum=down_momentum, tables_first=tables_first, tables_second=tables_second, time_first=time_first, time_second=time_second, mod_first=mod_first, mod_second=mod_second, adam_step=adam_step)


@jax.custom_vjp
def low(v):
    return lax.optimization_barrier(v.astype(jnp.bfloat16)).astype(jnp.float32)

@jax.custom_vjp
def low_back(v):
    return v

def low_keep(v):
    return (low(v), None)

def low_pass(kept, grad):
    return (grad,)

def back_keep(v):
    return (v, None)

def back_low(kept, grad):
    return (low(grad),)
low.defvjp(low_keep, low_pass)
low_back.defvjp(back_keep, back_low)
highest = lax.Precision.HIGHEST
beta_one = 0.5
beta_two = 0.95
adam_eps = 1e-08
adam_decay = 0.01
rate_tables = 0.05
rate_time = 0.01
rate_modulation = 0.02
muon_mu = 0.5
muon_rate = 1.0
muon_decay = 0.01
clip_norm = 0.001
ns_a = 3.4445
ns_b = -4.775
ns_c = 2.0315

def freq_table(time_index):
    half_width = FREQ // 2
    rates = jnp.exp(-math.log(10000.0) * jnp.arange(half_width, dtype=jnp.float32) / half_width)
    time_value = (time_index.astype(jnp.float32) + 0.5) * (1000.0 / TSTEPS)
    angles = time_value[:, None] * rates[None, :]
    return jnp.concatenate([jnp.cos(angles), jnp.sin(angles)], axis=1)

def position_table():
    quarter = D // 4
    omega_rates = 1.0 / 10000.0 ** (jnp.arange(quarter, dtype=jnp.float32) / quarter)
    positions = jnp.arange(TOK)
    col_angle = (positions % GRID).astype(jnp.float32)[:, None] * omega_rates[None, :]
    row_angle = (positions // GRID).astype(jnp.float32)[:, None] * omega_rates[None, :]
    return jnp.concatenate([jnp.sin(col_angle), jnp.cos(col_angle), jnp.sin(row_angle), jnp.cos(row_angle)], axis=1)

def layer_norm(stream):
    centered = stream - lax.optimization_barrier(jnp.mean(stream, axis=-1, keepdims=True))
    return centered * lax.rsqrt(lax.optimization_barrier(jnp.mean(centered * centered, axis=-1, keepdims=True)) + 1e-06)

def forward_loss(weights, latents, noise, labels, time_index):
    tables, time_proj, modulation, qkv_proj, out_proj, up_proj, down_proj = [low(weight) for weight in weights]
    patch_w = tables[:PATCH_IN]
    time_in = tables[PATCH_IN:PATCH_IN + FREQ]
    class_table = tables[PATCH_IN + FREQ:PATCH_IN + FREQ + CLASSES]
    head_t = tables[PATCH_IN + FREQ + CLASSES:]
    freq = low(freq_table(time_index))
    time_pre = low_back(jnp.dot(freq, time_in, precision=highest))
    time_act = low(jax.nn.silu(time_pre))
    condition = low_back(jnp.dot(time_act, time_proj, precision=highest) + class_table[labels])
    cond_act = low(jax.nn.silu(condition))
    mods = low_back(jnp.dot(cond_act, modulation, precision=highest))
    time_value = (time_index.astype(jnp.float32) + 0.5) / TSTEPS
    group = SEQ_MB * MICRO
    blocks = SEQS // group
    position = position_table()

    def one_block(summed, pieces):
        latent_rows, noise_rows, time_rows, mod_rows = pieces
        times = time_rows[:, None, None]
        noisy = (1.0 - times) * latent_rows + times * noise_rows
        target = noise_rows - latent_rows
        stream = low_back(jnp.einsum('gtp,pd->gtd', low(noisy), patch_w, precision=highest)) + position[None]
        for layer_index in range(LAYERS):
            layer_mods = mod_rows[:, layer_index * 6 * D:(layer_index + 1) * 6 * D].reshape(group, 6, D)
            shift_a, scale_a, gate_a, shift_b, scale_b, gate_b = [layer_mods[:, slot, None, :] for slot in range(6)]
            in_a = low(layer_norm(stream) * (1.0 + scale_a) + shift_a)
            qkv = low(low_back(jnp.einsum('gtd,dcm->gtcm', in_a, qkv_proj[layer_index], precision=highest)))
            queries = qkv[:, :, 0].reshape(group, TOK, HEADS, HD)
            key_rows = qkv[:, :, 1].reshape(group, TOK, HEADS, HD)
            values = qkv[:, :, 2].reshape(group, TOK, HEADS, HD)
            scores = low_back(jnp.einsum('gqhd,gkhd->ghqk', queries, key_rows, precision=highest) * HD ** (-0.5))
            probs = low(jax.nn.softmax(scores, axis=-1))
            attended = low(low_back(jnp.einsum('ghqk,gkhd->gqhd', probs, values, precision=highest).reshape(group, TOK, D)))
            branch_a = low_back(jnp.einsum('gtm,md->gtd', attended, out_proj[layer_index], precision=highest))
            stream = stream + gate_a * branch_a
            in_b = low(layer_norm(stream) * (1.0 + scale_b) + shift_b)
            hidden_pre = low_back(jnp.einsum('gtd,df->gtf', in_b, up_proj[layer_index], precision=highest))
            hidden = low(jax.nn.gelu(hidden_pre, approximate=True))
            branch_b = low_back(jnp.einsum('gtf,fd->gtd', hidden, down_proj[layer_index], precision=highest))
            stream = stream + gate_b * branch_b
        base = 6 * LAYERS * D
        shift_f = mod_rows[:, None, base:base + D]
        scale_f = mod_rows[:, None, base + D:base + 2 * D]
        in_f = low(layer_norm(stream) * (1.0 + scale_f) + shift_f)
        output = low_back(jnp.einsum('gtd,pd->gtp', in_f, head_t, precision=highest))
        miss = output - target
        return (summed + jnp.sum((0.5 + times) * miss * miss), None)
    pieces = (latents.reshape(blocks, group, TOK, PATCH_IN), noise.reshape(blocks, group, TOK, PATCH_IN), time_value.reshape(blocks, group), mods.reshape(blocks, group, MODW))
    summed, unused = lax.scan(jax.checkpoint(one_block), jnp.zeros((), jnp.float32), pieces)
    return summed / (SEQS * TOK * PATCH_IN)

def orthogonalize(matrix):
    matrix = matrix / (jnp.sqrt(jnp.sum(matrix * matrix)) + 1e-07)
    for iteration in range(NS_ITERS):
        gram = jnp.dot(matrix, matrix.T, precision=highest)
        poly_term = ns_b * gram + ns_c * jnp.dot(gram, gram, precision=highest)
        matrix = ns_a * matrix + jnp.dot(poly_term, matrix, precision=highest)
    return matrix

def muon_update(weight, gradient, momentum, orient, restore, shape_scale):
    momentum_new = muon_mu * momentum + gradient
    nesterov = gradient + muon_mu * momentum_new
    ortho = jnp.stack([restore(orthogonalize(orient(nesterov[layer_index]))) for layer_index in range(LAYERS)])
    return (weight * (1.0 - muon_rate * muon_decay) - muon_rate * shape_scale * ortho, momentum_new)

def adam_update(weight, gradient, first, second, rate, step_value):
    first_new = beta_one * first + (1.0 - beta_one) * gradient
    second_new = beta_two * second + (1.0 - beta_two) * gradient * gradient
    first_hat = first_new / (1.0 - jnp.power(beta_one, step_value))
    second_hat = second_new / (1.0 - jnp.power(beta_two, step_value))
    updated = weight * (1.0 - rate * adam_decay) - rate * first_hat / (jnp.sqrt(second_hat) + adam_eps)
    return (updated, first_new, second_new)

def reference(latents, noise, labels, time_index, tables, time_proj, modulation, qkv_proj, out_proj, up_proj, down_proj, qkv_momentum, out_momentum, up_momentum, down_momentum, tables_first, tables_second, time_first, time_second, mod_first, mod_second, adam_step):
    weights = (tables, time_proj, modulation, qkv_proj, out_proj, up_proj, down_proj)
    latent_rows = latents.astype(jnp.float32)
    noise_rows = noise.astype(jnp.float32)
    loss, pullback = jax.vjp(lambda params: forward_loss(params, latent_rows, noise_rows, labels, time_index), weights)
    gradients = pullback(jnp.ones((), jnp.float32))[0]
    square = sum((jnp.sum(gradient * gradient) for gradient in gradients))
    grad_norm = jnp.sqrt(square)
    factor = jnp.minimum(1.0, clip_norm / (grad_norm + 1e-06))
    grad_tables, grad_time, grad_mod, grad_qkv, grad_out, grad_up, grad_down = [gradient * factor for gradient in gradients]
    step_value = adam_step[0].astype(jnp.float32)
    qkv_updated, qkv_momentum_new = muon_update(qkv_proj, grad_qkv, qkv_momentum, lambda matrix: matrix.reshape(D, 3 * D), lambda matrix: matrix.reshape(D, 3, D), 1.0)
    out_updated, out_momentum_new = muon_update(out_proj, grad_out, out_momentum, lambda matrix: matrix.T, lambda matrix: matrix.T, 1.0)
    up_updated, up_momentum_new = muon_update(up_proj, grad_up, up_momentum, lambda matrix: matrix, lambda matrix: matrix, 1.0)
    down_updated, down_momentum_new = muon_update(down_proj, grad_down, down_momentum, lambda matrix: matrix.T, lambda matrix: matrix.T, math.sqrt(max(1.0, FF / D)))
    tables_updated, tables_first_new, tables_second_new = adam_update(tables, grad_tables, tables_first, tables_second, rate_tables, step_value)
    time_updated, time_first_new, time_second_new = adam_update(time_proj, grad_time, time_first, time_second, rate_time, step_value)
    mod_updated, mod_first_new, mod_second_new = adam_update(modulation, grad_mod, mod_first, mod_second, rate_modulation, step_value)
    return (loss, grad_norm, qkv_updated, qkv_momentum_new, out_updated, out_momentum_new, up_updated, up_momentum_new, down_updated, down_momentum_new, tables_updated, tables_first_new, tables_second_new, time_updated, time_first_new, time_second_new, mod_updated, mod_first_new, mod_second_new)
```

```python
import math

import jax
import jax.numpy as jnp
from jax import lax
from jax.experimental import pallas as pl
from jax.experimental.pallas import tpu as pltpu
from jax.sharding import Mesh
from jax.sharding import PartitionSpec as P

D = 768
FF = 3072
PATCH_IN = 16
FREQ = 256
CLASSES = 1000
GRID = 16
LAYERS = 2
NS_ITERS = 5
TSTEPS = 1000
HD = 64
TOK = 256


highest = lax.Precision.HIGHEST
DP = ("dh", "dm", "pr")
ALL = ("dh", "dm", "pr", "mp")
MATS = ("dh", "mp", "dm", "pr")
beta_one = 0.5
beta_two = 0.95
adam_eps = 1e-08
adam_decay = 0.01
rate_tables = 0.05
rate_time = 0.01
rate_modulation = 0.02
muon_mu = 0.5
muon_rate = 1.0
muon_decay = 0.01
clip_norm = 0.001
ns_a = 3.4445
ns_b = -4.775
ns_c = 2.0315


def freq_table(time_index):
    half_width = FREQ // 2
    rates = jnp.exp(-math.log(10000.0) * jnp.arange(half_width, dtype=jnp.float32) / half_width)
    time_value = (time_index.astype(jnp.float32) + 0.5) * (1000.0 / TSTEPS)
    angles = time_value[:, None] * rates[None, :]
    return jnp.concatenate([jnp.cos(angles), jnp.sin(angles)], axis=1)


def position_table():
    quarter = D // 4
    omega_rates = 1.0 / 10000.0 ** (jnp.arange(quarter, dtype=jnp.float32) / quarter)
    positions = jnp.arange(TOK)
    col_angle = (positions % GRID).astype(jnp.float32)[:, None] * omega_rates[None, :]
    row_angle = (positions // GRID).astype(jnp.float32)[:, None] * omega_rates[None, :]
    return jnp.concatenate(
        [jnp.sin(col_angle), jnp.cos(col_angle), jnp.sin(row_angle), jnp.cos(row_angle)], axis=1
    )


def layer_norm(stream):
    centered = stream - jnp.mean(stream, axis=-1, keepdims=True)
    inv_scale = lax.rsqrt(jnp.mean(centered * centered, axis=-1, keepdims=True) + 1e-06)
    return (centered * inv_scale, inv_scale)


def norm_back(normed, inv_scale, gradient):
    return inv_scale * (
        gradient
        - jnp.mean(gradient, axis=-1, keepdims=True)
        - normed * jnp.mean(gradient * normed, axis=-1, keepdims=True)
    )


def axis_bits(axis):
    return [(axis, bit) for bit in reversed(range(int(math.log2(lax.axis_size(axis)))))]


def own_bit(stage):
    axis, bit = stage
    return (lax.axis_index(axis) >> bit) & 1


def swap(value, stage):
    axis, bit = stage
    return lax.ppermute(
        value, axis, [(place, place ^ (1 << bit)) for place in range(lax.axis_size(axis))]
    )


def exchange_sum(value, stages):
    for stage in stages:
        value = value + swap(value, stage)
    return value


def exchange_gather(piece, stages):
    for stage in stages:
        piece = jnp.stack([piece, swap(piece, stage)])
    return piece


def own_places():
    return jnp.stack([lax.axis_index(axis) for axis in ALL]).astype(jnp.int32)


def turned(index, stage, places):
    axis, bit = stage
    return index ^ ((places[ALL.index(axis)] >> bit) & 1)


def block_places(part, stages, places):
    return tuple(
        turned((part >> bit) & 1, (axis, bit), places) if axis == "mp" else 0
        for axis, bit in stages
    ) + (0, 0)


def row_place(row, stages, places, sizes):
    parts = {"pr": row & 1, "dm": (row >> 1) % sizes["dm"], "dh": (row >> 1) // sizes["dm"]}
    return tuple(
        0 if axis == "mp" else turned((parts[axis] >> bit) & 1, (axis, bit), places)
        for axis, bit in stages
    )


def assemble(own_half, other_half, stages):
    mp_count = lax.axis_size("mp")
    sizes = {axis: lax.axis_size(axis) for axis in DP}
    pairs = sizes["dh"] * sizes["dm"]
    dims = stages[::-1]
    rows, cols = own_half.shape[-2:]
    block = tuple(1 if axis == "mp" else 2 for axis, bit in dims) + (rows, cols)

    def kernel(places, own_ref, other_ref, out_ref):
        source = pl.program_id(0)
        for pair in range(pairs):
            place = row_place(2 * pair, dims, places, sizes)

            @pl.when(source == 0)
            def _():
                out_ref[0, pair, 0] = own_ref[place]

            @pl.when(source == 1)
            def _():
                out_ref[0, pair, 0] = other_ref[place]

    return pl.pallas_call(
        kernel,
        out_shape=jax.ShapeDtypeStruct((mp_count, pairs, 2, rows, cols), own_half.dtype),
        grid_spec=pltpu.PrefetchScalarGridSpec(
            num_scalar_prefetch=1,
            grid=(2, mp_count),
            in_specs=[
                pl.BlockSpec(
                    block,
                    lambda source, part, places: block_places(
                        jnp.where(source == 0, part, mp_count - 1), dims, places
                    ),
                ),
                pl.BlockSpec(
                    block,
                    lambda source, part, places: block_places(
                        jnp.where(source == 1, part, 0), dims, places
                    ),
                ),
            ],
            out_specs=pl.BlockSpec(
                (1, pairs, 1, rows, cols),
                lambda source, part, places: (part, 0, source ^ places[2], 0, 0),
            ),
        ),
        cost_estimate=pl.CostEstimate(
            flops=0, transcendentals=0, bytes_accessed=8 * own_half.size
        ),
        name="assemble",
    )(own_places(), own_half, other_half)


def weight_grads(lefts, right, edge, stages):
    mp_count, tok_count, cols = right.shape
    sizes = {axis: lax.axis_size(axis) for axis in DP}
    pairs = sizes["dh"] * sizes["dm"]
    dims = stages[::-1]
    width = lefts[0].shape[0]
    rows = width // (2 * pairs)
    block = tuple(1 if axis == "mp" else 2 for axis, bit in dims) + (rows, cols)
    shape = jax.ShapeDtypeStruct((2,) * len(dims) + (rows, cols), jnp.float32)

    def kernel(places, *refs):
        left_refs = refs[: len(lefts)]
        right_ref, kept_ref, sent_ref, total_ref = refs[len(lefts) :]
        right_part = right_ref[0]
        total = jnp.dot(left_refs[0][...], right_part, preferred_element_type=jnp.float32)
        if len(lefts) > 1:
            second = jnp.dot(left_refs[1][...], right_part, preferred_element_type=jnp.float32)
            column = lax.broadcasted_iota(jnp.int32, total.shape, 1)
            total = jnp.where(column < edge, total, second)
        for row in range(2 * pairs):
            total_ref[row] = total[row * rows : (row + 1) * rows]
        for pair in range(pairs):
            place = row_place(2 * pair, dims, places, sizes)
            kept_ref[place] = total_ref[2 * pair + places[2]]
            sent_ref[place] = total_ref[2 * pair + 1 - places[2]]

    spec = pl.BlockSpec(block, lambda part, places: block_places(part, dims, places))
    return pl.pallas_call(
        kernel,
        out_shape=(shape, shape),
        grid_spec=pltpu.PrefetchScalarGridSpec(
            num_scalar_prefetch=1,
            grid=(mp_count,),
            in_specs=[
                pl.BlockSpec((width, tok_count), lambda part, places: (0, 0)) for left in lefts
            ]
            + [pl.BlockSpec((1, tok_count, cols), lambda part, places: (part, 0, 0))],
            out_specs=(spec, spec),
            scratch_shapes=[pltpu.VMEM((2 * pairs, rows, cols), jnp.float32)],
        ),
        cost_estimate=pl.CostEstimate(
            flops=2 * mp_count * width * tok_count * cols,
            transcendentals=0,
            bytes_accessed=4 * mp_count * width * cols,
        ),
        name="weight_grads",
    )(own_places(), *lefts, right)


def exchange_reduce(kept, sent, stages, wide):
    total = kept + swap(sent, ("pr", 0))
    for stage in stages[::-1]:
        sent = total[1]
        if not (wide and stage[0] == "mp"):
            sent = sent.astype(jnp.bfloat16)
        total = total[0] + swap(sent, stage).astype(jnp.float32)
    return total


def slow_gather(piece):
    piece = lax.all_gather(lax.all_gather(piece, DP, axis=0, tiled=True), "mp", axis=0)
    return piece


def slow_reduce(lefts, right, edge):
    total = jnp.einsum("dt,jtn->jdn", lefts[0], right, preferred_element_type=jnp.float32)
    if len(lefts) > 1:
        second = jnp.einsum("dt,jtn->jdn", lefts[1], right, preferred_element_type=jnp.float32)
        total = jnp.concatenate([total[..., :edge], second[..., edge:]], axis=-1)
    total = lax.psum_scatter(total, "mp", scatter_dimension=0, tiled=False)
    return lax.psum_scatter(total, DP, scatter_dimension=0, tiled=True)


def attend(queries, key_rows, values):
    scores = jnp.einsum(
        "sqhd,skhd->shqk", queries, key_rows, preferred_element_type=jnp.float32
    ) * HD ** (-0.5)
    row_peak = jnp.max(scores, axis=-1, keepdims=True)
    exponent = jnp.exp(scores - row_peak)
    row_total = jnp.sum(exponent, axis=-1, keepdims=True)
    probs = (exponent / row_total).astype(jnp.bfloat16)
    attended = jnp.einsum(
        "shqk,skhd->sqhd", probs, values, preferred_element_type=jnp.float32
    ).astype(jnp.bfloat16)
    return (attended, row_peak + jnp.log(row_total))


def attend_back(queries, key_rows, values, log_total, grad_heads):
    scores = jnp.einsum(
        "sqhd,skhd->shqk", queries, key_rows, preferred_element_type=jnp.float32
    ) * HD ** (-0.5)
    probs = jnp.exp(scores - log_total)
    probs_low = probs.astype(jnp.bfloat16)
    d_values = jnp.einsum(
        "shqk,sqhd->skhd", probs_low, grad_heads, preferred_element_type=jnp.float32
    )
    d_probs = jnp.einsum("sqhd,skhd->shqk", grad_heads, values, preferred_element_type=jnp.float32)
    d_scores = (probs * (d_probs - jnp.sum(d_probs * probs, axis=-1, keepdims=True))).astype(
        jnp.bfloat16
    )
    d_queries = jnp.einsum(
        "shqk,skhd->sqhd", d_scores, key_rows, preferred_element_type=jnp.float32
    ) * HD ** (-0.5)
    d_keys = jnp.einsum(
        "shqk,sqhd->skhd", d_scores, queries, preferred_element_type=jnp.float32
    ) * HD ** (-0.5)
    return (
        d_queries.astype(jnp.bfloat16),
        d_keys.astype(jnp.bfloat16),
        d_values.astype(jnp.bfloat16),
    )


def head_split(qkv):
    seq_count, tok_count, parts, width = qkv.shape
    third = width // 3
    return [
        qkv[..., slot * third : (slot + 1) * third].reshape(
            seq_count, tok_count, parts * third // HD, HD
        )
        for slot in range(3)
    ]


def layer_forward(stream, layer_weights, layer_mods):
    w_qkv, w_out, w_up, w_down = layer_weights
    shift_a, scale_a, gate_a, shift_b, scale_b, gate_b = [
        layer_mods[:, slot, None, :] for slot in range(6)
    ]
    seq_count, tok_count = stream.shape[:2]
    normed_a, inv_a = layer_norm(stream)
    in_a = (normed_a * (1.0 + scale_a) + shift_a).astype(jnp.bfloat16)
    qkv = jnp.einsum("std,jdn->stjn", in_a, w_qkv, preferred_element_type=jnp.float32).astype(
        jnp.bfloat16
    )
    heads = head_split(qkv)
    attended, log_total = attend(*heads)
    attended = attended.reshape(seq_count, tok_count, w_out.shape[0], w_out.shape[2])
    branch_a = jnp.einsum("stjm,jdm->std", attended, w_out, preferred_element_type=jnp.float32)
    stream_mid = stream + gate_a * branch_a
    normed_b, inv_b = layer_norm(stream_mid)
    in_b = (normed_b * (1.0 + scale_b) + shift_b).astype(jnp.bfloat16)
    hidden_pre = jnp.einsum("std,jdf->stjf", in_b, w_up, preferred_element_type=jnp.float32)
    hidden = jax.nn.gelu(hidden_pre, approximate=True).astype(jnp.bfloat16)
    branch_b = jnp.einsum("stjf,jdf->std", hidden, w_down, preferred_element_type=jnp.float32)
    saved_layer = (
        normed_a,
        inv_a,
        in_a,
        heads,
        log_total,
        attended,
        branch_a,
        normed_b,
        inv_b,
        in_b,
        hidden_pre,
        hidden,
        branch_b,
    )
    return (stream_mid + gate_b * branch_b, saved_layer)


def layer_backward(gradient, saved_layer, layer_weights, layer_mods):
    w_qkv, w_out, w_up, w_down = layer_weights
    (
        normed_a,
        inv_a,
        in_a,
        heads,
        log_total,
        attended,
        branch_a,
        normed_b,
        inv_b,
        in_b,
        hidden_pre,
        hidden,
        branch_b,
    ) = saved_layer
    shift_a, scale_a, gate_a, shift_b, scale_b, gate_b = [
        layer_mods[:, slot, None, :] for slot in range(6)
    ]
    seq_count, tok_count = gradient.shape[:2]
    low = jnp.bfloat16
    d_branch_b = (gate_b * gradient).astype(low)
    d_gate_b = jnp.sum(gradient * branch_b, axis=1)
    d_hidden = jnp.einsum("std,jdf->stjf", d_branch_b, w_down, preferred_element_type=jnp.float32)
    d_pre = jax.vjp(lambda value_in: jax.nn.gelu(value_in, approximate=True), hidden_pre)[1](
        d_hidden
    )[0].astype(low)
    d_in_b = jnp.einsum("stjf,jdf->std", d_pre, w_up, preferred_element_type=jnp.float32)
    d_scale_b = jnp.sum(d_in_b * normed_b, axis=1)
    d_shift_b = jnp.sum(d_in_b, axis=1)
    d_mid = gradient + norm_back(normed_b, inv_b, d_in_b * (1.0 + scale_b))
    d_branch_a = (gate_a * d_mid).astype(low)
    d_gate_a = jnp.sum(d_mid * branch_a, axis=1)
    d_attended = jnp.einsum(
        "std,jdm->stjm", d_branch_a, w_out, preferred_element_type=jnp.float32
    ).astype(low)
    parts = w_out.shape[0]
    d_heads = attend_back(*heads, log_total, d_attended.reshape(heads[0].shape))
    d_qkv = jnp.concatenate(
        [piece.reshape(seq_count, tok_count, parts, -1) for piece in d_heads], axis=-1
    )
    d_in_a = jnp.einsum("stjn,jdn->std", d_qkv, w_qkv, preferred_element_type=jnp.float32)
    d_scale_a = jnp.sum(d_in_a * normed_a, axis=1)
    d_shift_a = jnp.sum(d_in_a, axis=1)
    grad_in = d_mid + norm_back(normed_a, inv_a, d_in_a * (1.0 + scale_a))
    d_mods = jnp.stack([d_shift_a, d_scale_a, d_gate_a, d_shift_b, d_scale_b, d_gate_b], axis=1)

    def flat(value):
        return value.reshape((seq_count * tok_count,) + value.shape[2:])

    def parted(value):
        return flat(value).transpose(1, 0, 2)

    factors = (
        ((flat(in_b).T,), parted(d_pre)),
        ((flat(d_branch_b).T,), parted(hidden)),
        (
            (flat(in_a).T, flat(d_branch_a).T),
            parted(jnp.concatenate([d_qkv, attended], axis=-1)),
        ),
    )
    return (grad_in, d_mods, factors)


def polar_factor(gram):
    width = gram.shape[0]
    eye = jnp.eye(width, dtype=jnp.float32)
    frobenius = jnp.sqrt(jnp.trace(gram)) + 1e-07
    square = gram / (frobenius * frobenius)
    total = None
    for iteration in range(NS_ITERS):
        poly = ns_a * eye + ns_b * square + ns_c * mat_dot(square, square)
        total = poly if total is None else mat_dot(poly, total)
        if iteration < NS_ITERS - 1:
            square = mat_dot(mat_dot(poly, square), poly)
    return total / frobenius


def mat_dot(left, right):
    return jnp.dot(left, right, precision=lax.Precision.HIGH)


def adam_update(weight, gradient, first, second, rate, step_value):
    first_new = beta_one * first + (1.0 - beta_one) * gradient
    second_new = beta_two * second + (1.0 - beta_two) * gradient * gradient
    first_hat = first_new / (1.0 - jnp.power(beta_one, step_value))
    second_hat = second_new / (1.0 - jnp.power(beta_two, step_value))
    updated = weight * (1.0 - rate * adam_decay) - rate * first_hat / (
        jnp.sqrt(second_hat) + adam_eps
    )
    return (updated, first_new, second_new)


def body(
    latents,
    noise,
    labels,
    time_index,
    tables,
    time_proj,
    modulation,
    qkv_proj,
    out_proj,
    up_proj,
    down_proj,
    qkv_momentum,
    out_momentum,
    up_momentum,
    down_momentum,
    tables_first,
    tables_second,
    time_first,
    time_second,
    mod_first,
    mod_second,
    adam_step,
):
    low = jnp.bfloat16
    mp_count = lax.axis_size("mp")
    dp_count = lax.axis_size(DP)
    mp_own = lax.axis_index("mp")
    dp_own = lax.axis_index(DP)
    row_count = qkv_proj.shape[1]
    width_qkv = 3 * qkv_proj.shape[3]
    width_out = out_proj.shape[1]
    dp_stages = axis_bits("dh") + axis_bits("dm") + axis_bits("pr")
    mp_stages = axis_bits("mp")
    order = mp_stages + dp_stages
    fast = row_count % 16 == 0
    y_stages, x_stages = (axis_bits("dh"), axis_bits("dm")[::-1])
    routes = [
        [
            mp_stages + y_stages + x_stages,
            first + mp_stages + last,
            mp_stages + x_stages + y_stages,
        ]
        for first, last in ((x_stages, y_stages), (y_stages, x_stages))
    ]
    assert LAYERS == len(routes)

    def gather_whole(piece, stages):
        if not fast:
            return slow_gather(piece)
        piece = exchange_gather(piece, stages)
        return assemble(piece, swap(piece, ("pr", 0)), stages)

    def reduce_whole(lefts, right, stages, wide):
        if not fast:
            return slow_reduce(lefts, right, width_qkv)
        kept, sent = weight_grads(lefts, right, width_qkv, stages)
        return exchange_reduce(kept, sent, stages, wide)

    def oriented(qkv, out, up, down):
        layers = []
        for layer_index in range(LAYERS):
            layers.append(
                (
                    up[layer_index],
                    down[layer_index].T,
                    jnp.concatenate(
                        [qkv[layer_index].reshape(row_count, width_qkv), out[layer_index].T], axis=1
                    ),
                )
            )
        return layers

    def restored(layers):
        up = jnp.stack([pieces[0] for pieces in layers])
        down = jnp.stack([pieces[1].T for pieces in layers])
        qkv = jnp.stack(
            [pieces[2][:, :width_qkv].reshape(row_count, 3, width_qkv // 3) for pieces in layers]
        )
        out = jnp.stack([pieces[2][:, width_qkv:].T for pieces in layers])
        return (qkv, out, up, down)

    gathered = []
    for pieces in oriented(
        qkv_proj.astype(low), out_proj.astype(low), up_proj.astype(low), down_proj.astype(low)
    ):
        up_all, down_all, rest_all = [
            gather_whole(piece, stages).reshape(mp_count, dp_count * row_count, piece.shape[1])
            for piece, stages in zip(pieces, routes[len(gathered)])
        ]
        gathered.append(
            (rest_all[..., :width_qkv], rest_all[..., width_qkv:], up_all, down_all)
        )

    tables_low = tables.astype(low)
    time_low = time_proj.astype(low)
    mod_low = modulation.astype(low)
    time_in = tables_low[PATCH_IN : PATCH_IN + FREQ]
    class_table = tables_low[PATCH_IN + FREQ : PATCH_IN + FREQ + CLASSES]
    ends = jnp.concatenate([tables_low[:PATCH_IN], tables_low[PATCH_IN + FREQ + CLASSES :]], axis=0)
    index_rows = lax.all_gather(jnp.stack([labels, time_index]), DP, axis=1, tiled=True)
    every_label, every_time = (index_rows[0], index_rows[1])
    ends_all = lax.all_gather(ends, DP, axis=1, tiled=True)
    patch_w, head_t = (ends_all[:PATCH_IN], ends_all[PATCH_IN:])
    every_count = every_time.shape[0]
    freq = freq_table(every_time).astype(low)
    time_pre = jnp.dot(freq, time_in, preferred_element_type=jnp.float32)
    time_act = jax.nn.silu(time_pre).astype(low)
    onehot = (every_label[:, None] == jnp.arange(CLASSES)[None, :]).astype(low)
    time_part = jnp.dot(time_act, time_low, preferred_element_type=jnp.float32)
    time_part = time_part.reshape(every_count, dp_count, row_count).transpose(1, 0, 2)
    time_part = lax.all_to_all(time_part, DP, split_axis=0, concat_axis=0, tiled=True)
    condition = jnp.sum(time_part, axis=0) + jnp.dot(
        onehot, class_table, preferred_element_type=jnp.float32
    )
    cond_act = jax.nn.silu(condition).astype(low)
    mod_part = jnp.dot(cond_act, mod_low, preferred_element_type=jnp.float32)
    seq_count = every_count // (dp_count * mp_count)
    mod_width = mod_low.shape[1]
    mod_part = lax.all_to_all(mod_part, ALL, split_axis=0, concat_axis=0, tiled=True)
    mod_rows = jnp.sum(mod_part.reshape(dp_count, mp_count, seq_count, mod_width), axis=0)
    mod_rows = mod_rows.transpose(1, 0, 2).reshape(seq_count, mp_count * mod_width)

    first_row = mp_own * seq_count
    latent_rows = lax.dynamic_slice_in_dim(latents, first_row, seq_count, 0)
    noise_rows = lax.dynamic_slice_in_dim(noise, first_row, seq_count, 0)
    time_rows = lax.dynamic_slice_in_dim(time_index, first_row, seq_count, 0)
    token_count = every_count * TOK * PATCH_IN
    times = ((time_rows.astype(jnp.float32) + 0.5) / TSTEPS)[:, None, None]
    latents_f = latent_rows.astype(jnp.float32)
    noise_f = noise_rows.astype(jnp.float32)
    noisy = ((1.0 - times) * latents_f + times * noise_f).astype(low)
    target = noise_f - latents_f
    stream = (
        jnp.einsum("stp,pd->std", noisy, patch_w, preferred_element_type=jnp.float32)
        + position_table()[None]
    )
    layer_mods = [
        mod_rows[:, layer_index * 6 * D : (layer_index + 1) * 6 * D].reshape(seq_count, 6, D)
        for layer_index in range(LAYERS)
    ]
    saved_all = []
    for layer_index in range(LAYERS):
        stream, saved_layer = layer_forward(stream, gathered[layer_index], layer_mods[layer_index])
        saved_all.append(saved_layer)
    base = 6 * LAYERS * D
    shift_f = mod_rows[:, None, base : base + D]
    scale_f = mod_rows[:, None, base + D : base + 2 * D]
    normed_f, inv_f = layer_norm(stream)
    in_f = (normed_f * (1.0 + scale_f) + shift_f).astype(low)
    output = jnp.einsum("std,pd->stp", in_f, head_t, preferred_element_type=jnp.float32)
    weight_t = 0.5 + times
    velocity_miss = output - target
    loss_part = jnp.sum(weight_t * velocity_miss * velocity_miss) / token_count
    d_output = (2.0 * weight_t * velocity_miss / token_count).astype(low)
    d_head = jnp.einsum("stp,std->pd", d_output, in_f, preferred_element_type=jnp.float32)
    d_in_f = jnp.einsum("stp,pd->std", d_output, head_t, preferred_element_type=jnp.float32)
    d_scale_f = jnp.sum(d_in_f * normed_f, axis=1)
    d_shift_f = jnp.sum(d_in_f, axis=1)
    gradient = norm_back(normed_f, inv_f, d_in_f * (1.0 + scale_f))
    mod_grads = [None] * LAYERS
    layer_grads = [None] * LAYERS
    for layer_index in reversed(range(LAYERS)):
        gradient, d_mods, factors = layer_backward(
            gradient, saved_all[layer_index], gathered[layer_index], layer_mods[layer_index]
        )
        mod_grads[layer_index] = d_mods.reshape(seq_count, 6 * D)
        layer_grads[layer_index] = [
            reduce_whole(lefts, right, stages, len(lefts) > 1)
            for (lefts, right), stages in zip(factors, routes[layer_index])
        ]
    d_first = gradient.astype(low)
    d_patch = jnp.einsum("stp,std->pd", noisy, d_first, preferred_element_type=jnp.float32)
    d_ends = exchange_sum(jnp.concatenate([d_patch, d_head], axis=0), order[::-1])
    d_ends = lax.dynamic_slice_in_dim(d_ends, dp_own * row_count, row_count, 1)
    d_mod_all = jnp.concatenate(mod_grads + [d_shift_f, d_scale_f], axis=1).astype(low)
    d_mod_all = d_mod_all.reshape(seq_count, mp_count, mod_width).transpose(1, 0, 2)
    d_mod_sent = jnp.broadcast_to(
        d_mod_all[None], (dp_count, mp_count, seq_count, mod_width)
    ).reshape(every_count, mod_width)
    d_mod_own = lax.all_to_all(d_mod_sent, ALL, split_axis=0, concat_axis=0, tiled=True)
    grad_mod = jnp.einsum("sd,sm->dm", cond_act, d_mod_own, preferred_element_type=jnp.float32)
    d_cond_act = exchange_sum(
        jnp.einsum("sm,dm->sd", d_mod_own, mod_low, preferred_element_type=jnp.float32), mp_stages
    )
    d_condition = jax.vjp(jax.nn.silu, condition)[1](d_cond_act)[0].astype(low)
    d_class = jnp.einsum("sc,sd->cd", onehot, d_condition, preferred_element_type=jnp.float32)
    d_condition_all = lax.all_gather(d_condition, DP, axis=1, tiled=True)
    grad_time = jnp.einsum("se,sd->ed", time_act, d_condition_all, preferred_element_type=jnp.float32)
    d_time_act = jnp.einsum(
        "sd,ed->se", d_condition_all, time_low, preferred_element_type=jnp.float32
    )
    d_time_pre = jax.vjp(jax.nn.silu, time_pre)[1](d_time_act)[0].astype(low)
    d_time_in = jnp.einsum("sf,sd->fd", freq, d_time_pre, preferred_element_type=jnp.float32)
    grad_tables = jnp.concatenate(
        [d_ends[:PATCH_IN], d_time_in, d_class, d_ends[PATCH_IN:]], axis=0
    )

    shared_square = (jnp.sum(grad_tables * grad_tables) + jnp.sum(grad_time * grad_time)) / mp_count
    own_square = jnp.sum(grad_mod * grad_mod) + sum(
        jnp.sum(piece * piece) for pieces in layer_grads for piece in pieces
    )
    scalars = jnp.stack([shared_square + own_square, loss_part])
    scalars = jnp.broadcast_to(jnp.pad(scalars, (0, 126))[None], (8, 128))
    scalars = exchange_sum(scalars, order[::-1])
    square_total, loss = (scalars[0, 0], scalars[0, 1])
    grad_norm = jnp.sqrt(square_total)
    factor = jnp.minimum(1.0, clip_norm / (grad_norm + 1e-06))
    step_value = adam_step[0].astype(jnp.float32)
    tables_updated, tables_first_new, tables_second_new = adam_update(
        tables, grad_tables * factor, tables_first, tables_second, rate_tables, step_value
    )
    time_updated, time_first_new, time_second_new = adam_update(
        time_proj, grad_time * factor, time_first, time_second, rate_time, step_value
    )
    mod_updated, mod_first_new, mod_second_new = adam_update(
        modulation, grad_mod * factor, mod_first, mod_second, rate_modulation, step_value
    )

    momenta = oriented(qkv_momentum, out_momentum, up_momentum, down_momentum)
    momenta_new = [
        [muon_mu * momentum + factor * grad for momentum, grad in zip(old, new)]
        for old, new in zip(momenta, layer_grads)
    ]
    pushes = [
        [factor * grad + muon_mu * momentum for momentum, grad in zip(new_momentum, new)]
        for new_momentum, new in zip(momenta_new, layer_grads)
    ]
    group = dp_count // 2
    piece_cols = up_proj.shape[2] // group

    def cut(matrix):
        pieces = matrix.reshape(row_count, group, matrix.shape[1] // group)
        pieces = pieces.transpose(1, 0, 2)
        return jnp.pad(pieces, ((0, 0), (0, 0), (0, piece_cols - pieces.shape[2])))

    sent = []
    for up, down, rest in pushes:
        sent += [cut(up), cut(down), cut(rest[:, :width_qkv]), cut(rest[:, width_qkv:])]
    sent = jnp.stack(sent).reshape(dp_count * mp_count, row_count, piece_cols)
    got = lax.all_to_all(sent, MATS, split_axis=0, concat_axis=0, tiled=True)
    got = got.reshape(2, mp_count, group, row_count, piece_cols).transpose(0, 2, 3, 1, 4)
    matrix = got.reshape(2 * group * row_count, mp_count * piece_cols)
    gram = gram_sum(mat_dot(matrix, matrix.T))
    polar = polar_factor(gram)
    ortho = mat_dot(polar, matrix).astype(low)
    ortho = ortho.reshape(2, group, row_count, mp_count, piece_cols).transpose(0, 3, 1, 2, 4)
    ortho = ortho.reshape(dp_count * mp_count, row_count, piece_cols)
    back = lax.all_to_all(ortho, MATS, split_axis=0, concat_axis=0, tiled=True)
    back = back.reshape(4 * LAYERS, group, row_count, piece_cols)

    def joined(slot, width):
        pieces = back[slot][:, :, : width // group].transpose(1, 0, 2)
        return pieces.reshape(row_count, width).astype(jnp.float32)

    down_scale = math.sqrt(max(1.0, FF / D))
    ortho_layers = [
        (
            joined(4 * layer_index, up_proj.shape[2]),
            down_scale * joined(4 * layer_index + 1, up_proj.shape[2]),
            jnp.concatenate(
                [
                    joined(4 * layer_index + 2, width_qkv),
                    joined(4 * layer_index + 3, width_out),
                ],
                axis=1,
            ),
        )
        for layer_index in range(LAYERS)
    ]
    keep_factor = 1.0 - muon_rate * muon_decay
    updated = [
        weight * keep_factor - muon_rate * push
        for weight, push in zip((qkv_proj, out_proj, up_proj, down_proj), restored(ortho_layers))
    ]
    momenta_out = restored(momenta_new)
    return (
        loss,
        grad_norm,
        updated[0],
        momenta_out[0],
        updated[1],
        momenta_out[1],
        updated[2],
        momenta_out[2],
        updated[3],
        momenta_out[3],
        tables_updated,
        tables_first_new,
        tables_second_new,
        time_updated,
        time_first_new,
        time_second_new,
        mod_updated,
        mod_first_new,
        mod_second_new,
    )


def gram_sum(partial):
    half = partial.shape[0] // 2
    mine = lax.axis_index("pr")
    sent = lax.dynamic_slice_in_dim(partial, (1 - mine) * half, half, 0)
    kept = lax.dynamic_slice_in_dim(partial, mine * half, half, 0)
    kept = kept + swap(sent, ("pr", 0))
    kept = exchange_sum(kept, axis_bits("dm"))
    other_half = swap(kept, ("pr", 0))
    upper = mine == 1
    return jnp.concatenate(
        [jnp.where(upper, other_half, kept), jnp.where(upper, kept, other_half)], axis=0
    )


def solution(mesh):
    shape = mesh.devices.shape
    split = Mesh(mesh.devices.reshape(2, shape[0] // 4, 2, shape[1]), ALL)
    return jax.shard_map(
        body,
        mesh=split,
        in_specs=(
            P(DP, None, None),
            P(DP, None, None),
            P(DP),
            P(DP),
            P(None, DP),
            P(DP, None),
            P(DP, "mp"),
            P(None, DP, None, "mp"),
            P(None, "mp", DP),
            P(None, DP, "mp"),
            P(None, "mp", DP),
            P(None, DP, None, "mp"),
            P(None, "mp", DP),
            P(None, DP, "mp"),
            P(None, "mp", DP),
            P(None, DP),
            P(None, DP),
            P(DP, None),
            P(DP, None),
            P(DP, "mp"),
            P(DP, "mp"),
            P(),
        ),
        out_specs=(
            P(),
            P(),
            P(None, DP, None, "mp"),
            P(None, DP, None, "mp"),
            P(None, "mp", DP),
            P(None, "mp", DP),
            P(None, DP, "mp"),
            P(None, DP, "mp"),
            P(None, "mp", DP),
            P(None, "mp", DP),
            P(None, DP),
            P(None, DP),
            P(None, DP),
            P(DP, None),
            P(DP, None),
            P(DP, None),
            P(DP, "mp"),
            P(DP, "mp"),
            P(DP, "mp"),
        ),
        check_vma=False,
    )
```

```python
import math

import jax
import jax.numpy as jnp
from jax import lax
from jax.experimental import pallas as pl
from jax.experimental.pallas import tpu as pltpu
from jax.sharding import Mesh
from jax.sharding import PartitionSpec as P

D = 768
FF = 3072
PATCH_IN = 16
FREQ = 256
CLASSES = 1000
GRID = 16
LAYERS = 2
NS_ITERS = 5
TSTEPS = 1000
HD = 64
TOK = 256


highest = lax.Precision.HIGHEST
DP = ("dh", "dm", "pr")
ALL = ("dh", "dm", "pr", "mp")
MATS = ("dh", "mp", "dm", "pr")
beta_one = 0.5
beta_two = 0.95
adam_eps = 1e-08
adam_decay = 0.01
rate_tables = 0.05
rate_time = 0.01
rate_modulation = 0.02
muon_mu = 0.5
muon_rate = 1.0
muon_decay = 0.01
clip_norm = 0.001
ns_a = 3.4445
ns_b = -4.775
ns_c = 2.0315


def freq_table(time_index):
    half_width = FREQ // 2
    rates = jnp.exp(-math.log(10000.0) * jnp.arange(half_width, dtype=jnp.float32) / half_width)
    time_value = (time_index.astype(jnp.float32) + 0.5) * (1000.0 / TSTEPS)
    angles = time_value[:, None] * rates[None, :]
    return jnp.concatenate([jnp.cos(angles), jnp.sin(angles)], axis=1)


def position_table():
    quarter = D // 4
    omega_rates = 1.0 / 10000.0 ** (jnp.arange(quarter, dtype=jnp.float32) / quarter)
    positions = jnp.arange(TOK)
    col_angle = (positions % GRID).astype(jnp.float32)[:, None] * omega_rates[None, :]
    row_angle = (positions // GRID).astype(jnp.float32)[:, None] * omega_rates[None, :]
    return jnp.concatenate(
        [jnp.sin(col_angle), jnp.cos(col_angle), jnp.sin(row_angle), jnp.cos(row_angle)], axis=1
    )


def layer_norm(stream):
    centered = stream - jnp.mean(stream, axis=-1, keepdims=True)
    inv_scale = lax.rsqrt(jnp.mean(centered * centered, axis=-1, keepdims=True) + 1e-06)
    return (centered * inv_scale, inv_scale)


def norm_back(normed, inv_scale, gradient):
    return inv_scale * (
        gradient
        - jnp.mean(gradient, axis=-1, keepdims=True)
        - normed * jnp.mean(gradient * normed, axis=-1, keepdims=True)
    )


def axis_bits(axis):
    return [(axis, bit) for bit in reversed(range(int(math.log2(lax.axis_size(axis)))))]


def own_bit(stage):
    axis, bit = stage
    return (lax.axis_index(axis) >> bit) & 1


def swap(value, stage):
    axis, bit = stage
    return lax.ppermute(
        value, axis, [(place, place ^ (1 << bit)) for place in range(lax.axis_size(axis))]
    )


def exchange_sum(value, stages):
    for stage in stages:
        value = value + swap(value, stage)
    return value


def after(value, *others):
    return lax.optimization_barrier((value, others))[0]


def own_places():
    return jnp.stack([lax.axis_index(axis) for axis in ALL]).astype(jnp.int32)


def turned(index, stage, places):
    axis, bit = stage
    return index ^ ((places[ALL.index(axis)] >> bit) & 1)


def block_places(part, stages, places):
    return tuple(
        turned((part >> bit) & 1, (axis, bit), places) if axis == "mp" else 0
        for axis, bit in stages
    ) + (0, 0)


def row_place(row, stages, places, sizes):
    parts = {"pr": row & 1, "dm": (row >> 1) % sizes["dm"], "dh": (row >> 1) // sizes["dm"]}
    return tuple(
        0 if axis == "mp" else turned((parts[axis] >> bit) & 1, (axis, bit), places)
        for axis, bit in stages
    )


def mp_walk(dims):
    mp_dims = [bit for axis, bit in dims if axis == "mp"]

    def bit_of(step, stage):
        return (step >> (len(mp_dims) - 1 - mp_dims.index(stage[1]))) & 1

    def part_of(step, places):
        rel = sum(bit_of(step, ("mp", bit)) << bit for bit in mp_dims)
        return rel ^ places[3]

    def inner_place(step):
        return tuple(bit_of(step, stage) if stage[0] == "mp" else 0 for stage in dims[1:]) + (0, 0)

    return (bit_of, part_of, inner_place)


def assemble(pieces, stages, edges):
    mp_count = lax.axis_size("mp")
    sizes = {axis: lax.axis_size(axis) for axis in DP}
    pairs = sizes["dh"] * sizes["dm"]
    dims = stages[::-1]
    mp_first = dims[0][0] == "mp"
    bit_of, part_of, inner_place = mp_walk(dims)
    rows, cols = pieces[0].shape[-2:]
    block = tuple(1 if axis == "mp" else 2 for axis, bit in dims[1:]) + (rows, cols)
    widths = [last - first for first, last in zip(edges[:-1], edges[1:])]

    def kernel(places, *refs):
        piece_refs, out_refs = (refs[:4], refs[4:])
        source = pl.program_id(0)
        step = pl.program_id(1)
        for pair in range(pairs):
            place = row_place(2 * pair, dims, places, sizes)
            later = bit_of(step, dims[0]) if mp_first else place[0]
            for index in range(4):

                @pl.when((source == index // 2) & (later == index % 2))
                def _():
                    value = piece_refs[index][place[1:]]
                    for out_ref, first, last in zip(out_refs, edges[:-1], edges[1:]):
                        out_ref[0, pair, 0] = value[:, first:last]

    def in_spec(index):
        def place(source, step, places):
            now = jnp.where(source == index // 2, step, 0 if index // 2 else mp_count - 1)
            if mp_first:
                half = mp_count // 2
                now = jnp.maximum(now, half) if index % 2 else jnp.minimum(now, half - 1)
            return inner_place(now)

        return pl.BlockSpec(block, place)

    found = pl.pallas_call(
        kernel,
        out_shape=[
            jax.ShapeDtypeStruct((mp_count, pairs, 2, rows, width), pieces[0].dtype)
            for width in widths
        ],
        grid_spec=pltpu.PrefetchScalarGridSpec(
            num_scalar_prefetch=1,
            grid=(2, mp_count),
            in_specs=[in_spec(index) for index in range(4)],
            out_specs=[
                pl.BlockSpec(
                    (1, pairs, 1, rows, width),
                    lambda source, step, places: (
                        part_of(step, places),
                        0,
                        source ^ places[2],
                        0,
                        0,
                    ),
                )
                for width in widths
            ],
        ),
        cost_estimate=pl.CostEstimate(
            flops=0, transcendentals=0, bytes_accessed=16 * pieces[0].size
        ),
        name="assemble",
    )(own_places(), *pieces)
    return [piece.reshape(mp_count, pairs * 2 * rows, piece.shape[-1]) for piece in found]


def pair_factors(left, right):
    pairs = lax.axis_size("dh") * lax.axis_size("dm")
    width, tok_count = left.shape
    blocks = left.reshape(pairs, 2, width // (2 * pairs), tok_count)
    mine = lax.axis_index("pr")
    kept = lax.dynamic_index_in_dim(blocks, mine, 1, keepdims=False)
    sent = lax.dynamic_index_in_dim(blocks, 1 - mine, 1, keepdims=False)
    got = swap(sent, ("pr", 0))
    flat = (width // 2, tok_count)
    return (kept.reshape(flat), got.reshape(flat))


def weight_grads(lefts, rights, edge, stages):
    mp_count, tok_count, cols = rights[0].shape
    sizes = {axis: lax.axis_size(axis) for axis in DP}
    pairs = sizes["dh"] * sizes["dm"]
    dims = stages[::-1]
    width = lefts[0][0].shape[0]
    rows = width // pairs
    mp_first = dims[0][0] == "mp"
    bit_of, part_of, inner_place = mp_walk(dims)
    block = tuple(1 if axis == "mp" else 2 for axis, bit in dims[1:]) + (rows, cols)
    shape = (2,) * (len(dims) - 1) + (rows, cols)

    def kept_place(step, places):
        return inner_place(jnp.minimum(step, mp_count // 2 - 1) if mp_first else step)

    def sent_place(step, places):
        return inner_place(jnp.maximum(step, mp_count // 2) if mp_first else step)

    def kernel(places, *refs):
        left_refs = refs[: 2 * len(lefts)]
        right_refs, (kept_ref, sent_ref) = refs[2 * len(lefts) : -2], refs[-2:]
        step = pl.program_id(0)
        right_parts = [right_ref[0] for right_ref in right_refs]
        totals = [
            jnp.dot(
                left_refs[2 * index][...], right_parts[0], preferred_element_type=jnp.float32
            )
            + jnp.dot(
                left_refs[2 * index + 1][...], right_parts[1], preferred_element_type=jnp.float32
            )
            for index in range(len(lefts))
        ]
        total = totals[0]
        if len(lefts) > 1:
            column = lax.broadcasted_iota(jnp.int32, total.shape, 1)
            total = jnp.where(column < edge, total, totals[1])
        for pair in range(pairs):
            part = total[pair * rows : (pair + 1) * rows]
            place = row_place(2 * pair, dims, places, sizes)
            first = bit_of(step, dims[0]) if mp_first else place[0]

            @pl.when(first == 0)
            def _():
                kept_ref[place[1:]] = part

            @pl.when(first == 1)
            def _():
                sent_ref[place[1:]] = part.astype(jnp.bfloat16)

    left_spec = pl.BlockSpec((width, tok_count), lambda step, places: (0, 0))
    right_spec = pl.BlockSpec(
        (1, tok_count, cols), lambda step, places: (part_of(step, places), 0, 0)
    )
    return pl.pallas_call(
        kernel,
        out_shape=(
            jax.ShapeDtypeStruct(shape, jnp.float32),
            jax.ShapeDtypeStruct(shape, jnp.bfloat16),
        ),
        grid_spec=pltpu.PrefetchScalarGridSpec(
            num_scalar_prefetch=1,
            grid=(mp_count,),
            in_specs=[left_spec] * (2 * len(lefts)) + [right_spec] * 2,
            out_specs=(pl.BlockSpec(block, kept_place), pl.BlockSpec(block, sent_place)),
        ),
        cost_estimate=pl.CostEstimate(
            flops=4 * mp_count * width * tok_count * cols,
            transcendentals=0,
            bytes_accessed=6 * mp_count * width * cols,
        ),
        name="weight_grads",
    )(own_places(), *[left for couple in lefts for left in couple], *rights)


class Reduction:
    def __init__(self, kept, sent, stages, wide):
        self.stages = stages[::-1]
        self.wide = wide
        self.kept = kept
        self.sent = sent
        self.total = None

    def launch(self, sent):
        self.sent = None
        self.pending = swap(sent, self.stages[0])
        self.stages = self.stages[1:]

    def land(self):
        total = self.kept + self.pending.astype(jnp.float32)
        if self.stages:
            sent = total[1]
            if not (self.wide and self.stages[0][0] == "mp"):
                sent = sent.astype(jnp.bfloat16)
            self.kept, self.sent = (total[0], sent)
        else:
            self.total = total


def advance(value, active):
    for reduction in active:
        if reduction.sent is None and reduction.total is None:
            reduction.land()
    left = [reduction for reduction in active if reduction.sent is not None]
    value, sents = lax.optimization_barrier((value, [reduction.sent for reduction in left]))
    for reduction, sent in zip(left, sents):
        reduction.launch(sent)
    return value


def ordered_gather(piece, stages):
    for place, stage in enumerate(stages[::-1]):
        other_half = swap(piece, stage)
        upper = own_bit(stage) == 1
        piece = jnp.stack([jnp.where(upper, other_half, piece), jnp.where(upper, piece, other_half)])
        if place > 0:
            piece = piece.reshape((-1,) + piece.shape[2:])
    return piece


def slow_reduce(lefts, right, edge):
    total = jnp.einsum("dt,jtn->jdn", lefts[0], right, preferred_element_type=jnp.float32)
    if len(lefts) > 1:
        second = jnp.einsum("dt,jtn->jdn", lefts[1], right, preferred_element_type=jnp.float32)
        total = jnp.concatenate([total[..., :edge], second[..., edge:]], axis=-1)
    total = lax.psum_scatter(total, "mp", scatter_dimension=0, tiled=False)
    return lax.psum_scatter(total, DP, scatter_dimension=0, tiled=True)


def attend(queries, key_rows, values):
    scores = jnp.einsum(
        "jsqhd,jskhd->jshqk", queries, key_rows, preferred_element_type=jnp.float32
    ) * HD ** (-0.5)
    row_peak = jnp.max(scores, axis=-1, keepdims=True)
    exponent = jnp.exp(scores - row_peak)
    row_total = jnp.sum(exponent, axis=-1, keepdims=True)
    probs = (exponent / row_total).astype(jnp.bfloat16)
    attended = jnp.einsum(
        "jshqk,jskhd->jsqhd", probs, values, preferred_element_type=jnp.float32
    ).astype(jnp.bfloat16)
    return (attended, row_peak + jnp.log(row_total))


def attend_back(queries, key_rows, values, log_total, grad_heads):
    scores = jnp.einsum(
        "jsqhd,jskhd->jshqk", queries, key_rows, preferred_element_type=jnp.float32
    ) * HD ** (-0.5)
    probs = jnp.exp(scores - log_total)
    probs_low = probs.astype(jnp.bfloat16)
    d_values = jnp.einsum(
        "jshqk,jsqhd->jskhd", probs_low, grad_heads, preferred_element_type=jnp.float32
    )
    d_probs = jnp.einsum("jsqhd,jskhd->jshqk", grad_heads, values, preferred_element_type=jnp.float32)
    d_scores = (probs * (d_probs - jnp.sum(d_probs * probs, axis=-1, keepdims=True))).astype(
        jnp.bfloat16
    )
    d_queries = jnp.einsum(
        "jshqk,jskhd->jsqhd", d_scores, key_rows, preferred_element_type=jnp.float32
    ) * HD ** (-0.5)
    d_keys = jnp.einsum(
        "jshqk,jsqhd->jskhd", d_scores, queries, preferred_element_type=jnp.float32
    ) * HD ** (-0.5)
    return (
        d_queries.astype(jnp.bfloat16),
        d_keys.astype(jnp.bfloat16),
        d_values.astype(jnp.bfloat16),
    )


def head_split(qkv, seq_count):
    parts, rows, width = qkv.shape
    third = width // 3
    return [
        qkv[..., slot * third : (slot + 1) * third].reshape(
            parts, seq_count, rows // seq_count, third // HD, HD
        )
        for slot in range(3)
    ]


def tokens(value):
    return value.reshape((value.shape[0] * value.shape[1],) + value.shape[2:])


def product(spec, left, right):
    return jnp.einsum(spec, left, right, preferred_element_type=jnp.float32)


def layer_forward(stream, layer_weights, layer_mods, between):
    w_qkv, w_out, w_up, w_down = layer_weights
    shift_a, scale_a, gate_a, shift_b, scale_b, gate_b = [
        layer_mods[:, slot, None, :] for slot in range(6)
    ]
    low = jnp.bfloat16
    seq_count = stream.shape[0]
    normed_a, inv_a = layer_norm(stream)
    in_a = tokens((normed_a * (1.0 + scale_a) + shift_a).astype(low))
    qkv = product("td,jdn->jtn", in_a, w_qkv).astype(low)
    heads = head_split(qkv, seq_count)
    attended, log_total = attend(*heads)
    attended = attended.reshape(w_out.shape[0], in_a.shape[0], w_out.shape[2])
    branch_a = product("jtm,jdm->td", attended, w_out).reshape(stream.shape)
    stream_mid = between(stream + gate_a * branch_a)
    normed_b, inv_b = layer_norm(stream_mid)
    in_b = tokens((normed_b * (1.0 + scale_b) + shift_b).astype(low))
    hidden_pre = product("td,jdf->jtf", in_b, w_up)
    hidden = jax.nn.gelu(hidden_pre, approximate=True).astype(low)
    branch_b = product("jtf,jdf->td", hidden, w_down).reshape(stream.shape)
    saved_a = (normed_a, inv_a, in_a, heads, log_total, attended, branch_a)
    saved_b = (normed_b, inv_b, in_b, hidden_pre, hidden, branch_b)
    return (stream_mid + gate_b * branch_b, saved_a, saved_b)


def mlp_backward(gradient, saved_b, layer_weights, layer_mods):
    w_qkv, w_out, w_up, w_down = layer_weights
    normed_b, inv_b, in_b, hidden_pre, hidden, branch_b = saved_b
    scale_b, gate_b = [layer_mods[:, slot, None, :] for slot in (4, 5)]
    low = jnp.bfloat16
    d_branch_b = tokens((gate_b * gradient).astype(low))
    d_gate_b = jnp.sum(gradient * branch_b, axis=1)
    d_hidden = product("td,jdf->jtf", d_branch_b, w_down)
    d_pre = jax.vjp(lambda value_in: jax.nn.gelu(value_in, approximate=True), hidden_pre)[1](
        d_hidden
    )[0].astype(low)
    d_in_b = product("jtf,jdf->td", d_pre, w_up).reshape(gradient.shape)
    d_scale_b = jnp.sum(d_in_b * normed_b, axis=1)
    d_shift_b = jnp.sum(d_in_b, axis=1)
    d_mid = gradient + norm_back(normed_b, inv_b, d_in_b * (1.0 + scale_b))
    factors = (((in_b.T,), d_pre), ((d_branch_b.T,), hidden))
    return (d_mid, [d_shift_b, d_scale_b, d_gate_b], factors)


def attention_backward(d_mid, saved_a, layer_weights, layer_mods):
    w_qkv, w_out, w_up, w_down = layer_weights
    normed_a, inv_a, in_a, heads, log_total, attended, branch_a = saved_a
    scale_a, gate_a = [layer_mods[:, slot, None, :] for slot in (1, 2)]
    low = jnp.bfloat16
    d_branch_a = tokens((gate_a * d_mid).astype(low))
    d_gate_a = jnp.sum(d_mid * branch_a, axis=1)
    d_attended = product("td,jdm->jtm", d_branch_a, w_out).astype(low)
    d_heads = attend_back(*heads, log_total, d_attended.reshape(heads[0].shape))
    d_qkv = jnp.concatenate(
        [piece.reshape(attended.shape[:2] + (-1,)) for piece in d_heads], axis=-1
    )
    d_in_a = product("jtn,jdn->td", d_qkv, w_qkv).reshape(d_mid.shape)
    d_scale_a = jnp.sum(d_in_a * normed_a, axis=1)
    d_shift_a = jnp.sum(d_in_a, axis=1)
    grad_in = d_mid + norm_back(normed_a, inv_a, d_in_a * (1.0 + scale_a))
    factors = (((in_a.T, d_branch_a.T), jnp.concatenate([d_qkv, attended], axis=-1)),)
    return (grad_in, [d_shift_a, d_scale_a, d_gate_a], factors)


def polar_factor(gram):
    width = gram.shape[0]
    eye = jnp.eye(width, dtype=jnp.float32)
    frobenius = jnp.sqrt(jnp.trace(gram)) + 1e-07
    square = gram / (frobenius * frobenius)
    total = None
    for iteration in range(NS_ITERS):
        poly = ns_a * eye + ns_b * square + ns_c * mat_dot(square, square)
        total = poly if total is None else mat_dot(poly, total)
        if iteration < NS_ITERS - 1:
            square = mat_dot(mat_dot(poly, square), poly)
    return total / frobenius


def mat_dot(left, right):
    return jnp.dot(left, right, precision=lax.Precision.HIGH)


def adam_update(weight, gradient, first, second, rate, step_value):
    first_new = beta_one * first + (1.0 - beta_one) * gradient
    second_new = beta_two * second + (1.0 - beta_two) * gradient * gradient
    first_hat = first_new / (1.0 - jnp.power(beta_one, step_value))
    second_hat = second_new / (1.0 - jnp.power(beta_two, step_value))
    updated = weight * (1.0 - rate * adam_decay) - rate * first_hat / (
        jnp.sqrt(second_hat) + adam_eps
    )
    return (updated, first_new, second_new)


def body(
    latents,
    noise,
    labels,
    time_index,
    tables,
    time_proj,
    modulation,
    qkv_proj,
    out_proj,
    up_proj,
    down_proj,
    qkv_momentum,
    out_momentum,
    up_momentum,
    down_momentum,
    tables_first,
    tables_second,
    time_first,
    time_second,
    mod_first,
    mod_second,
    adam_step,
):
    low = jnp.bfloat16
    mp_count = lax.axis_size("mp")
    dp_count = lax.axis_size(DP)
    mp_own = lax.axis_index("mp")
    dp_own = lax.axis_index(DP)
    row_count = qkv_proj.shape[1]
    width_qkv = 3 * qkv_proj.shape[3]
    width_out = out_proj.shape[1]
    dp_stages = axis_bits("dh") + axis_bits("dm") + axis_bits("pr")
    mp_stages = axis_bits("mp")
    order = mp_stages + dp_stages
    fast = row_count % 16 == 0
    y_stages, x_stages = (axis_bits("dh"), axis_bits("dm")[::-1])
    routes = [
        y_stages + mp_stages + x_stages,
        x_stages + y_stages + mp_stages,
        mp_stages + x_stages + y_stages,
    ]
    edges = [(0, up_proj.shape[2]), (0, up_proj.shape[2]), (0, width_qkv, width_qkv + width_out)]

    def oriented(qkv, out, up, down):
        layers = []
        for layer_index in range(LAYERS):
            layers.append(
                (
                    up[layer_index],
                    down[layer_index].T,
                    jnp.concatenate(
                        [qkv[layer_index].reshape(row_count, width_qkv), out[layer_index].T], axis=1
                    ),
                )
            )
        return layers

    def restored(layers):
        up = jnp.stack([pieces[0] for pieces in layers])
        down = jnp.stack([pieces[1].T for pieces in layers])
        qkv = jnp.stack(
            [pieces[2][:, :width_qkv].reshape(row_count, 3, width_qkv // 3) for pieces in layers]
        )
        out = jnp.stack([pieces[2][:, width_qkv:].T for pieces in layers])
        return (qkv, out, up, down)

    def reduce_whole(lefts, right, stages, wide):
        couples = [pair_factors(left, right) for left in lefts]
        rights = (right, swap(right, ("pr", 0)))
        kept, sent = weight_grads(couples, rights, width_qkv, stages)
        return Reduction(kept, sent, stages, wide)

    shards = oriented(
        qkv_proj.astype(low), out_proj.astype(low), up_proj.astype(low), down_proj.astype(low)
    )
    pieces = [list(shard) for shard in shards]
    depths = [0] * LAYERS
    last_depth = len(routes[0]) - 1

    def gather_round(*layers):
        ready = lax.optimization_barrier([pieces[layer_index] for layer_index in layers])
        for layer_index, now in zip(layers, ready):
            depth = depths[layer_index]
            got = [swap(piece, stages[depth]) for piece, stages in zip(now, routes)]
            if depth < last_depth:
                pieces[layer_index] = [jnp.stack(both) for both in zip(now, got)]
            else:
                pieces[layer_index] = [
                    (own, other, swap(own, ("pr", 0)), swap(other, ("pr", 0)))
                    for own, other in zip(now, got)
                ]
            depths[layer_index] = depth + 1

    def whole(piece):
        piece = lax.all_gather(piece, ("mp",) + DP, axis=0, tiled=True)
        return piece.reshape(mp_count, dp_count * row_count, piece.shape[1])

    def layer_weights_of(layer_index):
        if not fast:
            up, down, rest = [whole(piece) for piece in pieces[layer_index]]
            return (rest[..., :width_qkv], rest[..., width_qkv:], up, down)
        found = [
            assemble(pieces[layer_index][slot], routes[slot], edges[slot]) for slot in (2, 0, 1)
        ]
        return found[0] + found[1] + found[2]

    def gather_dp(piece):
        if not fast:
            piece = lax.all_gather(piece, DP, axis=0)
        else:
            piece = ordered_gather(piece, dp_stages)
        return piece.transpose(1, 0, 2).reshape(piece.shape[1], -1)

    if fast:
        gather_round(0)

    tables_low = tables.astype(low)
    time_low = time_proj.astype(low)
    mod_low = modulation.astype(low)
    time_in = tables_low[PATCH_IN : PATCH_IN + FREQ]
    class_table = tables_low[PATCH_IN + FREQ : PATCH_IN + FREQ + CLASSES]
    ends = jnp.concatenate([tables_low[:PATCH_IN], tables_low[PATCH_IN + FREQ + CLASSES :]], axis=0)
    index_rows = gather_dp(jnp.stack([labels, time_index]))
    every_label, every_time = (index_rows[0], index_rows[1])
    ends_all = gather_dp(ends)
    patch_w, head_t = (ends_all[:PATCH_IN], ends_all[PATCH_IN:])
    every_count = every_time.shape[0]
    freq = freq_table(every_time).astype(low)
    time_pre = jnp.dot(freq, time_in, preferred_element_type=jnp.float32)
    time_act = jax.nn.silu(time_pre).astype(low)
    onehot = (every_label[:, None] == jnp.arange(CLASSES)[None, :]).astype(low)
    time_part = jnp.dot(time_act, time_low, preferred_element_type=jnp.float32)
    time_part = time_part.reshape(every_count, dp_count, row_count).transpose(1, 0, 2)
    time_part = lax.all_to_all(time_part, DP, split_axis=0, concat_axis=0, tiled=True)
    condition = jnp.sum(time_part, axis=0) + jnp.dot(
        onehot, class_table, preferred_element_type=jnp.float32
    )
    cond_act = jax.nn.silu(condition).astype(low)
    mod_part = jnp.dot(cond_act, mod_low, preferred_element_type=jnp.float32)
    seq_count = every_count // (dp_count * mp_count)
    mod_width = mod_low.shape[1]
    mod_part = lax.all_to_all(mod_part, ALL, split_axis=0, concat_axis=0, tiled=True)
    mod_rows = jnp.sum(mod_part.reshape(dp_count, mp_count, seq_count, mod_width), axis=0)
    mod_rows = mod_rows.transpose(1, 0, 2).reshape(seq_count, mp_count * mod_width)

    first_row = mp_own * seq_count
    latent_rows = lax.dynamic_slice_in_dim(latents, first_row, seq_count, 0)
    noise_rows = lax.dynamic_slice_in_dim(noise, first_row, seq_count, 0)
    time_rows = lax.dynamic_slice_in_dim(time_index, first_row, seq_count, 0)
    token_count = every_count * TOK * PATCH_IN
    times = ((time_rows.astype(jnp.float32) + 0.5) / TSTEPS)[:, None, None]
    latents_f = latent_rows.astype(jnp.float32)
    noise_f = noise_rows.astype(jnp.float32)
    noisy = ((1.0 - times) * latents_f + times * noise_f).astype(low)
    target = noise_f - latents_f
    stream = (
        jnp.einsum("stp,pd->std", noisy, patch_w, preferred_element_type=jnp.float32)
        + position_table()[None]
    )
    layer_mods = [
        mod_rows[:, layer_index * 6 * D : (layer_index + 1) * 6 * D].reshape(seq_count, 6, D)
        for layer_index in range(LAYERS)
    ]
    saved_all = []
    weights_all = []
    if fast:
        gather_round(0)
        gather_round(0, 1)
        gather_round(0, 1)
        pieces[1] = after(pieces[1], [halves[1] for halves in pieces[0]])
        gather_round(1)

    def between(value):
        if fast and layer_index == 0:
            value, pieces[1] = lax.optimization_barrier((value, pieces[1]))
            gather_round(1)
        return value

    for layer_index in range(LAYERS):
        weights_all.append(layer_weights_of(layer_index))
        stream, saved_a, saved_b = layer_forward(
            stream, weights_all[layer_index], layer_mods[layer_index], between
        )
        saved_all.append((saved_a, saved_b))
    base = 6 * LAYERS * D
    shift_f = mod_rows[:, None, base : base + D]
    scale_f = mod_rows[:, None, base + D : base + 2 * D]
    normed_f, inv_f = layer_norm(stream)
    in_f = (normed_f * (1.0 + scale_f) + shift_f).astype(low)
    output = jnp.einsum("std,pd->stp", in_f, head_t, preferred_element_type=jnp.float32)
    weight_t = 0.5 + times
    velocity_miss = output - target
    loss_part = jnp.sum(weight_t * velocity_miss * velocity_miss) / token_count
    d_output = (2.0 * weight_t * velocity_miss / token_count).astype(low)
    d_head = jnp.einsum("stp,std->pd", d_output, in_f, preferred_element_type=jnp.float32)
    d_in_f = jnp.einsum("stp,pd->std", d_output, head_t, preferred_element_type=jnp.float32)
    d_scale_f = jnp.sum(d_in_f * normed_f, axis=1)
    d_shift_f = jnp.sum(d_in_f, axis=1)
    gradient = norm_back(normed_f, inv_f, d_in_f * (1.0 + scale_f))
    mod_grads = [None] * LAYERS
    layer_grads = [None] * LAYERS
    active = []

    def collect(factors, stages_of):
        found = []
        for (lefts, right), stages in zip(factors, stages_of):
            if fast:
                found.append(reduce_whole(lefts, right, stages, len(lefts) > 1))
            else:
                found.append(slow_reduce(lefts, right, width_qkv))
        return found

    for layer_index in reversed(range(LAYERS)):
        saved_a, saved_b = saved_all[layer_index]
        weights = weights_all[layer_index]
        d_mid, d_mods_b, factors = mlp_backward(
            gradient, saved_b, weights, layer_mods[layer_index]
        )
        found = collect(factors, routes[:2])
        active += found
        if fast:
            d_mid = advance(d_mid, active)
        gradient, d_mods_a, factors = attention_backward(
            d_mid, saved_a, weights, layer_mods[layer_index]
        )
        last = collect(factors, routes[2:])
        active += last
        if fast:
            gradient = advance(gradient, active)
        mod_grads[layer_index] = jnp.concatenate(d_mods_a + d_mods_b, axis=1)
        layer_grads[layer_index] = found + last
    if fast:
        mod_grads, (d_shift_f, d_scale_f, d_head) = after(
            (mod_grads, (d_shift_f, d_scale_f, d_head)), gradient
        )
        while any(reduction.total is None for reduction in active):
            advance((), active)
        layer_grads = [[reduction.total for reduction in found] for found in layer_grads]
    d_first = gradient.astype(low)
    d_patch = jnp.einsum("stp,std->pd", noisy, d_first, preferred_element_type=jnp.float32)
    d_ends = exchange_sum(jnp.concatenate([d_patch, d_head], axis=0), order[::-1])
    d_ends = lax.dynamic_slice_in_dim(d_ends, dp_own * row_count, row_count, 1)
    d_mod_all = jnp.concatenate(mod_grads + [d_shift_f, d_scale_f], axis=1).astype(low)
    d_mod_all = d_mod_all.reshape(seq_count, mp_count, mod_width).transpose(1, 0, 2)
    d_mod_sent = jnp.broadcast_to(
        d_mod_all[None], (dp_count, mp_count, seq_count, mod_width)
    ).reshape(every_count, mod_width)
    d_mod_own = lax.all_to_all(d_mod_sent, ALL, split_axis=0, concat_axis=0, tiled=True)
    grad_mod = jnp.einsum("sd,sm->dm", cond_act, d_mod_own, preferred_element_type=jnp.float32)
    d_cond_act = exchange_sum(
        jnp.einsum("sm,dm->sd", d_mod_own, mod_low, preferred_element_type=jnp.float32), mp_stages
    )
    d_condition = jax.vjp(jax.nn.silu, condition)[1](d_cond_act)[0].astype(low)
    d_class = jnp.einsum("sc,sd->cd", onehot, d_condition, preferred_element_type=jnp.float32)
    d_condition_all = gather_dp(d_condition)
    grad_time = jnp.einsum("se,sd->ed", time_act, d_condition_all, preferred_element_type=jnp.float32)
    d_time_act = jnp.einsum(
        "sd,ed->se", d_condition_all, time_low, preferred_element_type=jnp.float32
    )
    d_time_pre = jax.vjp(jax.nn.silu, time_pre)[1](d_time_act)[0].astype(low)
    d_time_in = jnp.einsum("sf,sd->fd", freq, d_time_pre, preferred_element_type=jnp.float32)
    grad_tables = jnp.concatenate(
        [d_ends[:PATCH_IN], d_time_in, d_class, d_ends[PATCH_IN:]], axis=0
    )

    shared_square = (jnp.sum(grad_tables * grad_tables) + jnp.sum(grad_time * grad_time)) / mp_count
    own_square = jnp.sum(grad_mod * grad_mod) + sum(
        jnp.sum(piece * piece) for pieces in layer_grads for piece in pieces
    )
    scalars = jnp.stack([shared_square + own_square, loss_part])
    scalars = jnp.broadcast_to(jnp.pad(scalars, (0, 126))[None], (8, 128))
    scalars = exchange_sum(scalars, order[::-1])
    square_total, loss = (scalars[0, 0], scalars[0, 1])
    grad_norm = jnp.sqrt(square_total)
    factor = jnp.minimum(1.0, clip_norm / (grad_norm + 1e-06))
    step_value = adam_step[0].astype(jnp.float32)
    tables_updated, tables_first_new, tables_second_new = adam_update(
        tables, grad_tables * factor, tables_first, tables_second, rate_tables, step_value
    )
    time_updated, time_first_new, time_second_new = adam_update(
        time_proj, grad_time * factor, time_first, time_second, rate_time, step_value
    )
    mod_updated, mod_first_new, mod_second_new = adam_update(
        modulation, grad_mod * factor, mod_first, mod_second, rate_modulation, step_value
    )

    momenta = oriented(qkv_momentum, out_momentum, up_momentum, down_momentum)
    momenta_new = [
        [muon_mu * momentum + factor * grad for momentum, grad in zip(old, new)]
        for old, new in zip(momenta, layer_grads)
    ]
    pushes = [
        [factor * grad + muon_mu * momentum for momentum, grad in zip(new_momentum, new)]
        for new_momentum, new in zip(momenta_new, layer_grads)
    ]
    group = dp_count // 2
    piece_cols = up_proj.shape[2] // group

    def cut(matrix):
        pieces = matrix.reshape(row_count, group, matrix.shape[1] // group)
        pieces = pieces.transpose(1, 0, 2)
        return jnp.pad(pieces, ((0, 0), (0, 0), (0, piece_cols - pieces.shape[2])))

    sent = []
    for up, down, rest in pushes:
        sent += [cut(up), cut(down), cut(rest[:, :width_qkv]), cut(rest[:, width_qkv:])]
    sent = jnp.stack(sent).reshape(dp_count * mp_count, row_count, piece_cols)
    got = lax.all_to_all(sent, MATS, split_axis=0, concat_axis=0, tiled=True)
    got = got.reshape(2, mp_count, group, row_count, piece_cols).transpose(0, 2, 3, 1, 4)
    matrix = got.reshape(2 * group * row_count, mp_count * piece_cols)
    gram = gram_sum(mat_dot(matrix, matrix.T))
    polar = polar_factor(gram)
    ortho = mat_dot(polar, matrix).astype(low)
    ortho = ortho.reshape(2, group, row_count, mp_count, piece_cols).transpose(0, 3, 1, 2, 4)
    ortho = ortho.reshape(dp_count * mp_count, row_count, piece_cols)
    back = lax.all_to_all(ortho, MATS, split_axis=0, concat_axis=0, tiled=True)
    back = back.reshape(4 * LAYERS, group, row_count, piece_cols)

    def joined(slot, width):
        pieces = back[slot][:, :, : width // group].transpose(1, 0, 2)
        return pieces.reshape(row_count, width).astype(jnp.float32)

    down_scale = math.sqrt(max(1.0, FF / D))
    ortho_layers = [
        (
            joined(4 * layer_index, up_proj.shape[2]),
            down_scale * joined(4 * layer_index + 1, up_proj.shape[2]),
            jnp.concatenate(
                [
                    joined(4 * layer_index + 2, width_qkv),
                    joined(4 * layer_index + 3, width_out),
                ],
                axis=1,
            ),
        )
        for layer_index in range(LAYERS)
    ]
    keep_factor = 1.0 - muon_rate * muon_decay
    updated = [
        weight * keep_factor - muon_rate * push
        for weight, push in zip((qkv_proj, out_proj, up_proj, down_proj), restored(ortho_layers))
    ]
    momenta_out = restored(momenta_new)
    return (
        loss,
        grad_norm,
        updated[0],
        momenta_out[0],
        updated[1],
        momenta_out[1],
        updated[2],
        momenta_out[2],
        updated[3],
        momenta_out[3],
        tables_updated,
        tables_first_new,
        tables_second_new,
        time_updated,
        time_first_new,
        time_second_new,
        mod_updated,
        mod_first_new,
        mod_second_new,
    )


def gram_sum(partial):
    half = partial.shape[0] // 2
    mine = lax.axis_index("pr")
    sent = lax.dynamic_slice_in_dim(partial, (1 - mine) * half, half, 0)
    kept = lax.dynamic_slice_in_dim(partial, mine * half, half, 0)
    kept = kept + swap(sent, ("pr", 0))
    kept = exchange_sum(kept, axis_bits("dm"))
    other_half = swap(kept, ("pr", 0))
    upper = mine == 1
    return jnp.concatenate(
        [jnp.where(upper, other_half, kept), jnp.where(upper, kept, other_half)], axis=0
    )


def solution(mesh):
    shape = mesh.devices.shape
    split = Mesh(mesh.devices.reshape(2, shape[0] // 4, 2, shape[1]), ALL)
    return jax.shard_map(
        body,
        mesh=split,
        in_specs=(
            P(DP, None, None),
            P(DP, None, None),
            P(DP),
            P(DP),
            P(None, DP),
            P(DP, None),
            P(DP, "mp"),
            P(None, DP, None, "mp"),
            P(None, "mp", DP),
            P(None, DP, "mp"),
            P(None, "mp", DP),
            P(None, DP, None, "mp"),
            P(None, "mp", DP),
            P(None, DP, "mp"),
            P(None, "mp", DP),
            P(None, DP),
            P(None, DP),
            P(DP, None),
            P(DP, None),
            P(DP, "mp"),
            P(DP, "mp"),
            P(),
        ),
        out_specs=(
            P(),
            P(),
            P(None, DP, None, "mp"),
            P(None, DP, None, "mp"),
            P(None, "mp", DP),
            P(None, "mp", DP),
            P(None, DP, "mp"),
            P(None, DP, "mp"),
            P(None, "mp", DP),
            P(None, "mp", DP),
            P(None, DP),
            P(None, DP),
            P(None, DP),
            P(DP, None),
            P(DP, None),
            P(DP, None),
            P(DP, "mp"),
            P(DP, "mp"),
            P(DP, "mp"),
        ),
        check_vma=False,
    )
```

```python
import math

import jax
import jax.numpy as jnp
from jax import lax
from jax.experimental import pallas as pl
from jax.experimental.pallas import tpu as pltpu
from jax.sharding import Mesh
from jax.sharding import PartitionSpec as P

D = 768
FF = 3072
PATCH_IN = 16
FREQ = 256
CLASSES = 1000
GRID = 16
LAYERS = 2
NS_ITERS = 5
TSTEPS = 1000
HD = 64
TOK = 256


highest = lax.Precision.HIGHEST
DP = ("dh", "dm", "pr")
ALL = ("dh", "dm", "pr", "mp")
MATS = ("dh", "mp", "dm", "pr")
beta_one = 0.5
beta_two = 0.95
adam_eps = 1e-08
adam_decay = 0.01
rate_tables = 0.05
rate_time = 0.01
rate_modulation = 0.02
muon_mu = 0.5
muon_rate = 1.0
muon_decay = 0.01
clip_norm = 0.001
ns_a = 3.4445
ns_b = -4.775
ns_c = 2.0315


def freq_table(time_index):
    half_width = FREQ // 2
    rates = jnp.exp(-math.log(10000.0) * jnp.arange(half_width, dtype=jnp.float32) / half_width)
    time_value = (time_index.astype(jnp.float32) + 0.5) * (1000.0 / TSTEPS)
    angles = time_value[:, None] * rates[None, :]
    return jnp.concatenate([jnp.cos(angles), jnp.sin(angles)], axis=1)


def position_table():
    quarter = D // 4
    omega_rates = 1.0 / 10000.0 ** (jnp.arange(quarter, dtype=jnp.float32) / quarter)
    positions = jnp.arange(TOK)
    col_angle = (positions % GRID).astype(jnp.float32)[:, None] * omega_rates[None, :]
    row_angle = (positions // GRID).astype(jnp.float32)[:, None] * omega_rates[None, :]
    return jnp.concatenate(
        [jnp.sin(col_angle), jnp.cos(col_angle), jnp.sin(row_angle), jnp.cos(row_angle)], axis=1
    )


def layer_norm(stream):
    centered = stream - jnp.mean(stream, axis=-1, keepdims=True)
    inv_scale = lax.rsqrt(jnp.mean(centered * centered, axis=-1, keepdims=True) + 1e-06)
    return (centered * inv_scale, inv_scale)


def norm_back(normed, inv_scale, gradient):
    return inv_scale * (
        gradient
        - jnp.mean(gradient, axis=-1, keepdims=True)
        - normed * jnp.mean(gradient * normed, axis=-1, keepdims=True)
    )


def axis_bits(axis):
    return [(axis, bit) for bit in reversed(range(int(math.log2(lax.axis_size(axis)))))]


def own_bit(stage):
    axis, bit = stage
    return (lax.axis_index(axis) >> bit) & 1


def swap(value, stage):
    axis, bit = stage
    return lax.ppermute(
        value, axis, [(place, place ^ (1 << bit)) for place in range(lax.axis_size(axis))]
    )


def exchange_sum(value, stages):
    for stage in stages:
        value = value + swap(value, stage)
    return value


def after(value, *others):
    return lax.optimization_barrier((value, others))[0]


def own_places():
    return jnp.stack([lax.axis_index(axis) for axis in ALL]).astype(jnp.int32)


def turned(index, stage, places):
    axis, bit = stage
    return index ^ ((places[ALL.index(axis)] >> bit) & 1)


def block_places(part, stages, places):
    return tuple(
        turned((part >> bit) & 1, (axis, bit), places) if axis == "mp" else 0
        for axis, bit in stages
    ) + (0, 0)


def row_place(row, stages, places, sizes):
    parts = {"pr": row & 1, "dm": (row >> 1) % sizes["dm"], "dh": (row >> 1) // sizes["dm"]}
    return tuple(
        0 if axis == "mp" else turned((parts[axis] >> bit) & 1, (axis, bit), places)
        for axis, bit in stages
    )


def mp_walk(dims):
    mp_dims = [bit for axis, bit in dims if axis == "mp"]

    def bit_of(step, stage):
        return (step >> (len(mp_dims) - 1 - mp_dims.index(stage[1]))) & 1

    def part_of(step, places):
        rel = sum(bit_of(step, ("mp", bit)) << bit for bit in mp_dims)
        return rel ^ places[3]

    def inner_place(step):
        return tuple(bit_of(step, stage) if stage[0] == "mp" else 0 for stage in dims[1:]) + (0, 0)

    return (bit_of, part_of, inner_place)


def assemble(pieces, stages, edges):
    mp_count = lax.axis_size("mp")
    sizes = {axis: lax.axis_size(axis) for axis in DP}
    pairs = sizes["dh"] * sizes["dm"]
    dims = stages[::-1]
    mp_first = dims[0][0] == "mp"
    bit_of, part_of, inner_place = mp_walk(dims)
    rows, cols = pieces[0].shape[-2:]
    block = tuple(1 if axis == "mp" else 2 for axis, bit in dims[1:]) + (rows, cols)
    widths = [last - first for first, last in zip(edges[:-1], edges[1:])]

    def kernel(places, *refs):
        piece_refs, out_refs = (refs[:4], refs[4:])
        source = pl.program_id(0)
        step = pl.program_id(1)
        for pair in range(pairs):
            place = row_place(2 * pair, dims, places, sizes)
            later = bit_of(step, dims[0]) if mp_first else place[0]
            for index in range(4):

                @pl.when((source == index // 2) & (later == index % 2))
                def _():
                    value = piece_refs[index][place[1:]]
                    for out_ref, first, last in zip(out_refs, edges[:-1], edges[1:]):
                        out_ref[0, pair, 0] = value[:, first:last]

    def in_spec(index):
        def place(source, step, places):
            now = jnp.where(source == index // 2, step, 0 if index // 2 else mp_count - 1)
            if mp_first:
                half = mp_count // 2
                now = jnp.maximum(now, half) if index % 2 else jnp.minimum(now, half - 1)
            return inner_place(now)

        return pl.BlockSpec(block, place)

    found = pl.pallas_call(
        kernel,
        out_shape=[
            jax.ShapeDtypeStruct((mp_count, pairs, 2, rows, width), pieces[0].dtype)
            for width in widths
        ],
        grid_spec=pltpu.PrefetchScalarGridSpec(
            num_scalar_prefetch=1,
            grid=(2, mp_count),
            in_specs=[in_spec(index) for index in range(4)],
            out_specs=[
                pl.BlockSpec(
                    (1, pairs, 1, rows, width),
                    lambda source, step, places: (
                        part_of(step, places),
                        0,
                        source ^ places[2],
                        0,
                        0,
                    ),
                )
                for width in widths
            ],
        ),
        cost_estimate=pl.CostEstimate(
            flops=0, transcendentals=0, bytes_accessed=16 * pieces[0].size
        ),
        name="assemble",
    )(own_places(), *pieces)
    return [piece.reshape(mp_count, pairs * 2 * rows, piece.shape[-1]) for piece in found]


def pair_factors(left, right):
    pairs = lax.axis_size("dh") * lax.axis_size("dm")
    width, tok_count = left.shape
    blocks = left.reshape(pairs, 2, width // (2 * pairs), tok_count)
    mine = lax.axis_index("pr")
    kept = lax.dynamic_index_in_dim(blocks, mine, 1, keepdims=False)
    sent = lax.dynamic_index_in_dim(blocks, 1 - mine, 1, keepdims=False)
    got = swap(sent, ("pr", 0))
    flat = (width // 2, tok_count)
    return (kept.reshape(flat), got.reshape(flat))


def weight_grads(lefts, rights, edge, stages):
    mp_count, tok_count, cols = rights[0].shape
    sizes = {axis: lax.axis_size(axis) for axis in DP}
    pairs = sizes["dh"] * sizes["dm"]
    dims = stages[::-1]
    width = lefts[0][0].shape[0]
    rows = width // pairs
    mp_first = dims[0][0] == "mp"
    bit_of, part_of, inner_place = mp_walk(dims)
    block = tuple(1 if axis == "mp" else 2 for axis, bit in dims[1:]) + (rows, cols)
    shape = (2,) * (len(dims) - 1) + (rows, cols)

    def kept_place(step, places):
        return inner_place(jnp.minimum(step, mp_count // 2 - 1) if mp_first else step)

    def sent_place(step, places):
        return inner_place(jnp.maximum(step, mp_count // 2) if mp_first else step)

    def kernel(places, *refs):
        left_refs = refs[: 2 * len(lefts)]
        right_refs, (kept_ref, sent_ref) = refs[2 * len(lefts) : -2], refs[-2:]
        step = pl.program_id(0)
        right_parts = [right_ref[0] for right_ref in right_refs]
        totals = [
            jnp.dot(
                left_refs[2 * index][...], right_parts[0], preferred_element_type=jnp.float32
            )
            + jnp.dot(
                left_refs[2 * index + 1][...], right_parts[1], preferred_element_type=jnp.float32
            )
            for index in range(len(lefts))
        ]
        total = totals[0]
        if len(lefts) > 1:
            column = lax.broadcasted_iota(jnp.int32, total.shape, 1)
            total = jnp.where(column < edge, total, totals[1])
        for pair in range(pairs):
            part = total[pair * rows : (pair + 1) * rows]
            place = row_place(2 * pair, dims, places, sizes)
            first = bit_of(step, dims[0]) if mp_first else place[0]

            @pl.when(first == 0)
            def _():
                kept_ref[place[1:]] = part

            @pl.when(first == 1)
            def _():
                sent_ref[place[1:]] = part.astype(jnp.bfloat16)

    left_spec = pl.BlockSpec((width, tok_count), lambda step, places: (0, 0))
    right_spec = pl.BlockSpec(
        (1, tok_count, cols), lambda step, places: (part_of(step, places), 0, 0)
    )
    return pl.pallas_call(
        kernel,
        out_shape=(
            jax.ShapeDtypeStruct(shape, jnp.float32),
            jax.ShapeDtypeStruct(shape, jnp.bfloat16),
        ),
        grid_spec=pltpu.PrefetchScalarGridSpec(
            num_scalar_prefetch=1,
            grid=(mp_count,),
            in_specs=[left_spec] * (2 * len(lefts)) + [right_spec] * 2,
            out_specs=(pl.BlockSpec(block, kept_place), pl.BlockSpec(block, sent_place)),
        ),
        cost_estimate=pl.CostEstimate(
            flops=4 * mp_count * width * tok_count * cols,
            transcendentals=0,
            bytes_accessed=6 * mp_count * width * cols,
        ),
        name="weight_grads",
    )(own_places(), *[left for couple in lefts for left in couple], *rights)


class Reduction:
    def __init__(self, kept, sent, stages, wide):
        self.stages = stages[::-1]
        self.wide = wide
        self.kept = kept
        self.sent = sent
        self.total = None

    def launch(self, sent):
        self.sent = None
        self.pending = swap(sent, self.stages[0])
        self.stages = self.stages[1:]

    def land(self):
        total = self.kept + self.pending.astype(jnp.float32)
        if self.stages:
            sent = total[1]
            if not (self.wide and self.stages[0][0] == "mp"):
                sent = sent.astype(jnp.bfloat16)
            self.kept, self.sent = (total[0], sent)
        else:
            self.total = total


def advance(value, active):
    for reduction in active:
        if reduction.sent is None and reduction.total is None:
            reduction.land()
    left = [reduction for reduction in active if reduction.sent is not None]
    value, sents = lax.optimization_barrier((value, [reduction.sent for reduction in left]))
    for reduction, sent in zip(left, sents):
        reduction.launch(sent)
    return value


def ordered_gather(piece, stages):
    for place, stage in enumerate(stages[::-1]):
        other_half = swap(piece, stage)
        upper = own_bit(stage) == 1
        piece = jnp.stack([jnp.where(upper, other_half, piece), jnp.where(upper, piece, other_half)])
        if place > 0:
            piece = piece.reshape((-1,) + piece.shape[2:])
    return piece


def slow_reduce(lefts, right, edge):
    total = jnp.einsum("dt,jtn->jdn", lefts[0], right, preferred_element_type=jnp.float32)
    if len(lefts) > 1:
        second = jnp.einsum("dt,jtn->jdn", lefts[1], right, preferred_element_type=jnp.float32)
        total = jnp.concatenate([total[..., :edge], second[..., edge:]], axis=-1)
    total = lax.psum_scatter(total, "mp", scatter_dimension=0, tiled=False)
    return lax.psum_scatter(total, DP, scatter_dimension=0, tiled=True)


def attend(queries, key_rows, values):
    scores = jnp.einsum(
        "jsqhd,jskhd->jshqk", queries, key_rows, preferred_element_type=jnp.float32
    ) * HD ** (-0.5)
    row_peak = jnp.max(scores, axis=-1, keepdims=True)
    exponent = jnp.exp(scores - row_peak)
    row_total = jnp.sum(exponent, axis=-1, keepdims=True)
    probs = (exponent / row_total).astype(jnp.bfloat16)
    attended = jnp.einsum(
        "jshqk,jskhd->jsqhd", probs, values, preferred_element_type=jnp.float32
    ).astype(jnp.bfloat16)
    return (attended, row_peak + jnp.log(row_total))


def attend_back(queries, key_rows, values, log_total, grad_heads):
    scores = jnp.einsum(
        "jsqhd,jskhd->jshqk", queries, key_rows, preferred_element_type=jnp.float32
    ) * HD ** (-0.5)
    probs = jnp.exp(scores - log_total)
    probs_low = probs.astype(jnp.bfloat16)
    d_values = jnp.einsum(
        "jshqk,jsqhd->jskhd", probs_low, grad_heads, preferred_element_type=jnp.float32
    )
    d_probs = jnp.einsum("jsqhd,jskhd->jshqk", grad_heads, values, preferred_element_type=jnp.float32)
    d_scores = (probs * (d_probs - jnp.sum(d_probs * probs, axis=-1, keepdims=True))).astype(
        jnp.bfloat16
    )
    d_queries = jnp.einsum(
        "jshqk,jskhd->jsqhd", d_scores, key_rows, preferred_element_type=jnp.float32
    ) * HD ** (-0.5)
    d_keys = jnp.einsum(
        "jshqk,jsqhd->jskhd", d_scores, queries, preferred_element_type=jnp.float32
    ) * HD ** (-0.5)
    return (
        d_queries.astype(jnp.bfloat16),
        d_keys.astype(jnp.bfloat16),
        d_values.astype(jnp.bfloat16),
    )


def head_split(qkv, seq_count):
    parts, rows, width = qkv.shape
    third = width // 3
    return [
        qkv[..., slot * third : (slot + 1) * third].reshape(
            parts, seq_count, rows // seq_count, third // HD, HD
        )
        for slot in range(3)
    ]


def tokens(value):
    return value.reshape((value.shape[0] * value.shape[1],) + value.shape[2:])


def product(spec, left, right):
    return jnp.einsum(spec, left, right, preferred_element_type=jnp.float32)


def layer_forward(stream, layer_weights, layer_mods, between):
    w_qkv, w_out, w_up, w_down = layer_weights
    shift_a, scale_a, gate_a, shift_b, scale_b, gate_b = [
        layer_mods[:, slot, None, :] for slot in range(6)
    ]
    low = jnp.bfloat16
    seq_count = stream.shape[0]
    normed_a, inv_a = layer_norm(stream)
    in_a = tokens((normed_a * (1.0 + scale_a) + shift_a).astype(low))
    qkv = product("td,jdn->jtn", in_a, w_qkv).astype(low)
    heads = head_split(qkv, seq_count)
    attended, log_total = attend(*heads)
    attended = attended.reshape(w_out.shape[0], in_a.shape[0], w_out.shape[2])
    branch_a = product("jtm,jdm->td", attended, w_out).reshape(stream.shape)
    stream_mid = between(stream + gate_a * branch_a)
    normed_b, inv_b = layer_norm(stream_mid)
    in_b = tokens((normed_b * (1.0 + scale_b) + shift_b).astype(low))
    hidden_pre = product("td,jdf->jtf", in_b, w_up)
    hidden = jax.nn.gelu(hidden_pre, approximate=True).astype(low)
    branch_b = product("jtf,jdf->td", hidden, w_down).reshape(stream.shape)
    saved_a = (normed_a, inv_a, in_a, heads, log_total, attended, branch_a)
    saved_b = (normed_b, inv_b, in_b, hidden_pre, hidden, branch_b)
    return (stream_mid + gate_b * branch_b, saved_a, saved_b)


def mlp_backward(gradient, saved_b, layer_weights, layer_mods):
    w_qkv, w_out, w_up, w_down = layer_weights
    normed_b, inv_b, in_b, hidden_pre, hidden, branch_b = saved_b
    scale_b, gate_b = [layer_mods[:, slot, None, :] for slot in (4, 5)]
    low = jnp.bfloat16
    d_branch_b = tokens((gate_b * gradient).astype(low))
    d_gate_b = jnp.sum(gradient * branch_b, axis=1)
    d_hidden = product("td,jdf->jtf", d_branch_b, w_down)
    d_pre = jax.vjp(lambda value_in: jax.nn.gelu(value_in, approximate=True), hidden_pre)[1](
        d_hidden
    )[0].astype(low)
    d_in_b = product("jtf,jdf->td", d_pre, w_up).reshape(gradient.shape)
    d_scale_b = jnp.sum(d_in_b * normed_b, axis=1)
    d_shift_b = jnp.sum(d_in_b, axis=1)
    d_mid = gradient + norm_back(normed_b, inv_b, d_in_b * (1.0 + scale_b))
    factors = (((in_b.T,), d_pre), ((d_branch_b.T,), hidden))
    return (d_mid, [d_shift_b, d_scale_b, d_gate_b], factors)


def attention_backward(d_mid, saved_a, layer_weights, layer_mods):
    w_qkv, w_out, w_up, w_down = layer_weights
    normed_a, inv_a, in_a, heads, log_total, attended, branch_a = saved_a
    scale_a, gate_a = [layer_mods[:, slot, None, :] for slot in (1, 2)]
    low = jnp.bfloat16
    d_branch_a = tokens((gate_a * d_mid).astype(low))
    d_gate_a = jnp.sum(d_mid * branch_a, axis=1)
    d_attended = product("td,jdm->jtm", d_branch_a, w_out).astype(low)
    d_heads = attend_back(*heads, log_total, d_attended.reshape(heads[0].shape))
    d_qkv = jnp.concatenate(
        [piece.reshape(attended.shape[:2] + (-1,)) for piece in d_heads], axis=-1
    )
    d_in_a = product("jtn,jdn->td", d_qkv, w_qkv).reshape(d_mid.shape)
    d_scale_a = jnp.sum(d_in_a * normed_a, axis=1)
    d_shift_a = jnp.sum(d_in_a, axis=1)
    grad_in = d_mid + norm_back(normed_a, inv_a, d_in_a * (1.0 + scale_a))
    factors = (((in_a.T, d_branch_a.T), jnp.concatenate([d_qkv, attended], axis=-1)),)
    return (grad_in, [d_shift_a, d_scale_a, d_gate_a], factors)


def polar_factor(gram):
    width = gram.shape[0]
    eye = jnp.eye(width, dtype=jnp.float32)
    frobenius = jnp.sqrt(jnp.trace(gram)) + 1e-07
    square = gram / (frobenius * frobenius)
    total = None
    for iteration in range(NS_ITERS):
        poly = ns_a * eye + ns_b * square + ns_c * mat_dot(square, square)
        total = poly if total is None else mat_dot(poly, total)
        if iteration < NS_ITERS - 1:
            square = mat_dot(mat_dot(poly, square), poly)
    return total / frobenius


def mat_dot(left, right):
    return jnp.dot(left, right, precision=lax.Precision.HIGH)


def adam_update(weight, gradient, first, second, rate, step_value):
    first_new = beta_one * first + (1.0 - beta_one) * gradient
    second_new = beta_two * second + (1.0 - beta_two) * gradient * gradient
    first_hat = first_new / (1.0 - jnp.power(beta_one, step_value))
    second_hat = second_new / (1.0 - jnp.power(beta_two, step_value))
    updated = weight * (1.0 - rate * adam_decay) - rate * first_hat / (
        jnp.sqrt(second_hat) + adam_eps
    )
    return (updated, first_new, second_new)


def body(
    latents,
    noise,
    labels,
    time_index,
    tables,
    time_proj,
    modulation,
    qkv_proj,
    out_proj,
    up_proj,
    down_proj,
    qkv_momentum,
    out_momentum,
    up_momentum,
    down_momentum,
    tables_first,
    tables_second,
    time_first,
    time_second,
    mod_first,
    mod_second,
    adam_step,
):
    low = jnp.bfloat16
    mp_count = lax.axis_size("mp")
    dp_count = lax.axis_size(DP)
    mp_own = lax.axis_index("mp")
    dp_own = lax.axis_index(DP)
    row_count = qkv_proj.shape[1]
    width_qkv = 3 * qkv_proj.shape[3]
    width_out = out_proj.shape[1]
    dp_stages = axis_bits("dh") + axis_bits("dm") + axis_bits("pr")
    mp_stages = axis_bits("mp")
    order = mp_stages + dp_stages
    fast = row_count % 16 == 0
    y_stages, x_stages = (axis_bits("dh"), axis_bits("dm")[::-1])
    routes = [
        y_stages + mp_stages + x_stages,
        x_stages + y_stages + mp_stages,
        mp_stages + x_stages + y_stages,
    ]
    edges = [(0, up_proj.shape[2]), (0, up_proj.shape[2]), (0, width_qkv, width_qkv + width_out)]

    def oriented(qkv, out, up, down):
        layers = []
        for layer_index in range(LAYERS):
            layers.append(
                (
                    up[layer_index],
                    down[layer_index].T,
                    jnp.concatenate(
                        [qkv[layer_index].reshape(row_count, width_qkv), out[layer_index].T], axis=1
                    ),
                )
            )
        return layers

    def restored(layers):
        up = jnp.stack([pieces[0] for pieces in layers])
        down = jnp.stack([pieces[1].T for pieces in layers])
        qkv = jnp.stack(
            [pieces[2][:, :width_qkv].reshape(row_count, 3, width_qkv // 3) for pieces in layers]
        )
        out = jnp.stack([pieces[2][:, width_qkv:].T for pieces in layers])
        return (qkv, out, up, down)

    def reduce_whole(lefts, right, stages, wide):
        couples = [pair_factors(left, right) for left in lefts]
        rights = (right, swap(right, ("pr", 0)))
        kept, sent = weight_grads(couples, rights, width_qkv, stages)
        return Reduction(kept, sent, stages, wide)

    shards = oriented(
        qkv_proj.astype(low), out_proj.astype(low), up_proj.astype(low), down_proj.astype(low)
    )
    pieces = [list(shard) for shard in shards]
    depths = [0] * LAYERS
    last_depth = len(routes[0]) - 1

    def gather_round(*layers):
        ready = lax.optimization_barrier([pieces[layer_index] for layer_index in layers])
        for layer_index, now in zip(layers, ready):
            depth = depths[layer_index]
            got = [swap(piece, stages[depth]) for piece, stages in zip(now, routes)]
            if depth < last_depth:
                pieces[layer_index] = [jnp.stack(both) for both in zip(now, got)]
            else:
                pieces[layer_index] = [
                    (own, other, swap(own, ("pr", 0)), swap(other, ("pr", 0)))
                    for own, other in zip(now, got)
                ]
            depths[layer_index] = depth + 1

    def whole(piece):
        piece = lax.all_gather(piece, ("mp",) + DP, axis=0, tiled=True)
        return piece.reshape(mp_count, dp_count * row_count, piece.shape[1])

    def layer_weights_of(layer_index):
        if not fast:
            up, down, rest = [whole(piece) for piece in pieces[layer_index]]
            return (rest[..., :width_qkv], rest[..., width_qkv:], up, down)
        found = [
            assemble(pieces[layer_index][slot], routes[slot], edges[slot]) for slot in (2, 0, 1)
        ]
        return found[0] + found[1] + found[2]

    def gather_dp(piece):
        if not fast:
            piece = lax.all_gather(piece, DP, axis=0)
        else:
            piece = ordered_gather(piece, dp_stages)
        return piece.transpose(1, 0, 2).reshape(piece.shape[1], -1)

    if fast:
        gather_round(0)

    tables_low = tables.astype(low)
    time_low = time_proj.astype(low)
    mod_low = modulation.astype(low)
    time_in = tables_low[PATCH_IN : PATCH_IN + FREQ]
    class_table = tables_low[PATCH_IN + FREQ : PATCH_IN + FREQ + CLASSES]
    ends = jnp.concatenate([tables_low[:PATCH_IN], tables_low[PATCH_IN + FREQ + CLASSES :]], axis=0)
    index_rows = gather_dp(jnp.stack([labels, time_index]))
    every_label, every_time = (index_rows[0], index_rows[1])
    ends_all = gather_dp(ends)
    patch_w, head_t = (ends_all[:PATCH_IN], ends_all[PATCH_IN:])
    every_count = every_time.shape[0]
    freq = freq_table(every_time).astype(low)
    time_pre = jnp.dot(freq, time_in, preferred_element_type=jnp.float32)
    time_act = jax.nn.silu(time_pre).astype(low)
    onehot = (every_label[:, None] == jnp.arange(CLASSES)[None, :]).astype(low)
    time_part = jnp.dot(time_act, time_low, preferred_element_type=jnp.float32)
    time_part = time_part.reshape(every_count, dp_count, row_count).transpose(1, 0, 2)
    time_part = lax.all_to_all(time_part, DP, split_axis=0, concat_axis=0, tiled=True)
    condition = jnp.sum(time_part, axis=0) + jnp.dot(
        onehot, class_table, preferred_element_type=jnp.float32
    )
    cond_act = jax.nn.silu(condition).astype(low)
    mod_part = jnp.dot(cond_act, mod_low, preferred_element_type=jnp.float32)
    seq_count = every_count // (dp_count * mp_count)
    mod_width = mod_low.shape[1]
    mod_part = lax.all_to_all(mod_part, ALL, split_axis=0, concat_axis=0, tiled=True)
    mod_rows = jnp.sum(mod_part.reshape(dp_count, mp_count, seq_count, mod_width), axis=0)
    mod_rows = mod_rows.transpose(1, 0, 2).reshape(seq_count, mp_count * mod_width)

    first_row = mp_own * seq_count
    latent_rows = lax.dynamic_slice_in_dim(latents, first_row, seq_count, 0)
    noise_rows = lax.dynamic_slice_in_dim(noise, first_row, seq_count, 0)
    time_rows = lax.dynamic_slice_in_dim(time_index, first_row, seq_count, 0)
    token_count = every_count * TOK * PATCH_IN
    times = ((time_rows.astype(jnp.float32) + 0.5) / TSTEPS)[:, None, None]
    latents_f = latent_rows.astype(jnp.float32)
    noise_f = noise_rows.astype(jnp.float32)
    noisy = ((1.0 - times) * latents_f + times * noise_f).astype(low)
    target = noise_f - latents_f
    stream = (
        jnp.einsum("stp,pd->std", noisy, patch_w, preferred_element_type=jnp.float32)
        + position_table()[None]
    )
    layer_mods = [
        mod_rows[:, layer_index * 6 * D : (layer_index + 1) * 6 * D].reshape(seq_count, 6, D)
        for layer_index in range(LAYERS)
    ]
    group = dp_count // 2
    piece_cols = up_proj.shape[2] // group
    momenta = oriented(qkv_momentum, out_momentum, up_momentum, down_momentum)

    def cut(matrix):
        pieces = matrix.reshape(row_count, group, matrix.shape[1] // group)
        pieces = pieces.transpose(1, 0, 2)
        return jnp.pad(pieces, ((0, 0), (0, 0), (0, piece_cols - pieces.shape[2])))

    def to_sent(layers):
        sent = []
        for layer in layers:
            up, down, rest = [piece.astype(low) for piece in layer]
            sent += [cut(up), cut(down), cut(rest[:, :width_qkv]), cut(rest[:, width_qkv:])]
        return jnp.stack(sent).reshape(dp_count * mp_count, row_count, piece_cols)

    def to_owner(sent):
        got = lax.all_to_all(sent, MATS, split_axis=0, concat_axis=0, tiled=True)
        got = got.reshape(2, mp_count, group, row_count, piece_cols).transpose(0, 2, 3, 1, 4)
        return got.reshape(2 * group * row_count, mp_count * piece_cols)

    sent_momentum = to_sent(momenta)
    saved_all = []
    weights_all = []
    if fast:
        gather_round(0)
        gather_round(0, 1)
        gather_round(0, 1)
        pieces[1] = after(pieces[1], [halves[1] for halves in pieces[0]])
        gather_round(1)

    def between(value):
        if fast and layer_index == 0:
            value, pieces[1] = lax.optimization_barrier((value, pieces[1]))
            gather_round(1)
        return value

    for layer_index in range(LAYERS):
        weights_all.append(layer_weights_of(layer_index))
        stream, saved_a, saved_b = layer_forward(
            stream, weights_all[layer_index], layer_mods[layer_index], between
        )
        saved_all.append((saved_a, saved_b))
        if layer_index == 0:
            stream, sent_momentum = lax.optimization_barrier((stream, sent_momentum))
            rows_momentum = to_owner(sent_momentum)
    stream, rows_momentum = lax.optimization_barrier((stream, rows_momentum))
    base = 6 * LAYERS * D
    shift_f = mod_rows[:, None, base : base + D]
    scale_f = mod_rows[:, None, base + D : base + 2 * D]
    normed_f, inv_f = layer_norm(stream)
    in_f = (normed_f * (1.0 + scale_f) + shift_f).astype(low)
    output = jnp.einsum("std,pd->stp", in_f, head_t, preferred_element_type=jnp.float32)
    weight_t = 0.5 + times
    velocity_miss = output - target
    loss_part = jnp.sum(weight_t * velocity_miss * velocity_miss) / token_count
    d_output = (2.0 * weight_t * velocity_miss / token_count).astype(low)
    d_head = jnp.einsum("stp,std->pd", d_output, in_f, preferred_element_type=jnp.float32)
    d_in_f = jnp.einsum("stp,pd->std", d_output, head_t, preferred_element_type=jnp.float32)
    d_scale_f = jnp.sum(d_in_f * normed_f, axis=1)
    d_shift_f = jnp.sum(d_in_f, axis=1)
    gradient = norm_back(normed_f, inv_f, d_in_f * (1.0 + scale_f))
    mod_grads = [None] * LAYERS
    layer_grads = [None] * LAYERS
    active = []

    def collect(factors, stages_of):
        found = []
        for (lefts, right), stages in zip(factors, stages_of):
            if fast:
                found.append(reduce_whole(lefts, right, stages, len(lefts) > 1))
            else:
                found.append(slow_reduce(lefts, right, width_qkv))
        return found

    for layer_index in reversed(range(LAYERS)):
        saved_a, saved_b = saved_all[layer_index]
        weights = weights_all[layer_index]
        d_mid, d_mods_b, factors = mlp_backward(
            gradient, saved_b, weights, layer_mods[layer_index]
        )
        found = collect(factors, routes[:2])
        active += found
        if fast:
            d_mid = advance(d_mid, active)
        gradient, d_mods_a, factors = attention_backward(
            d_mid, saved_a, weights, layer_mods[layer_index]
        )
        last = collect(factors, routes[2:])
        active += last
        if fast:
            gradient = advance(gradient, active)
        mod_grads[layer_index] = jnp.concatenate(d_mods_a + d_mods_b, axis=1)
        layer_grads[layer_index] = found + last
    if fast:
        mod_grads, (d_shift_f, d_scale_f, d_head) = after(
            (mod_grads, (d_shift_f, d_scale_f, d_head)), gradient
        )
        while any(reduction.total is None for reduction in active):
            advance((), active)
        layer_grads = [[reduction.total for reduction in found] for found in layer_grads]
    d_first = gradient.astype(low)
    d_patch = jnp.einsum("stp,std->pd", noisy, d_first, preferred_element_type=jnp.float32)
    d_ends = exchange_sum(jnp.concatenate([d_patch, d_head], axis=0), order[::-1])
    d_ends = lax.dynamic_slice_in_dim(d_ends, dp_own * row_count, row_count, 1)
    d_mod_all = jnp.concatenate(mod_grads + [d_shift_f, d_scale_f], axis=1).astype(low)
    d_mod_all = d_mod_all.reshape(seq_count, mp_count, mod_width).transpose(1, 0, 2)
    d_mod_sent = jnp.broadcast_to(
        d_mod_all[None], (dp_count, mp_count, seq_count, mod_width)
    ).reshape(every_count, mod_width)
    d_mod_own = lax.all_to_all(d_mod_sent, ALL, split_axis=0, concat_axis=0, tiled=True)
    grad_mod = jnp.einsum("sd,sm->dm", cond_act, d_mod_own, preferred_element_type=jnp.float32)
    d_cond_act = exchange_sum(
        jnp.einsum("sm,dm->sd", d_mod_own, mod_low, preferred_element_type=jnp.float32), mp_stages
    )
    d_condition = jax.vjp(jax.nn.silu, condition)[1](d_cond_act)[0].astype(low)
    d_class = jnp.einsum("sc,sd->cd", onehot, d_condition, preferred_element_type=jnp.float32)
    d_condition_all = gather_dp(d_condition)
    grad_time = jnp.einsum("se,sd->ed", time_act, d_condition_all, preferred_element_type=jnp.float32)
    d_time_act = jnp.einsum(
        "sd,ed->se", d_condition_all, time_low, preferred_element_type=jnp.float32
    )
    d_time_pre = jax.vjp(jax.nn.silu, time_pre)[1](d_time_act)[0].astype(low)
    d_time_in = jnp.einsum("sf,sd->fd", freq, d_time_pre, preferred_element_type=jnp.float32)
    grad_tables = jnp.concatenate(
        [d_ends[:PATCH_IN], d_time_in, d_class, d_ends[PATCH_IN:]], axis=0
    )

    shared_square = (jnp.sum(grad_tables * grad_tables) + jnp.sum(grad_time * grad_time)) / mp_count
    own_square = jnp.sum(grad_mod * grad_mod) + sum(
        jnp.sum(piece * piece) for pieces in layer_grads for piece in pieces
    )
    scalars = jnp.stack([shared_square + own_square, loss_part])
    scalars = jnp.broadcast_to(jnp.pad(scalars, (0, 126))[None], (8, 128))
    scalars, sent_grads = lax.optimization_barrier((scalars, to_sent(layer_grads)))
    rows_grad = to_owner(sent_grads)
    scalars = exchange_sum(scalars, order[::-1])
    scalars, rows_grad = lax.optimization_barrier((scalars, rows_grad))
    square_total, loss = (scalars[0, 0], scalars[0, 1])
    grad_norm = jnp.sqrt(square_total)
    factor = jnp.minimum(1.0, clip_norm / (grad_norm + 1e-06))
    step_value = adam_step[0].astype(jnp.float32)
    tables_updated, tables_first_new, tables_second_new = adam_update(
        tables, grad_tables * factor, tables_first, tables_second, rate_tables, step_value
    )
    time_updated, time_first_new, time_second_new = adam_update(
        time_proj, grad_time * factor, time_first, time_second, rate_time, step_value
    )
    mod_updated, mod_first_new, mod_second_new = adam_update(
        modulation, grad_mod * factor, mod_first, mod_second, rate_modulation, step_value
    )

    momenta_new = [
        [muon_mu * momentum + factor * grad for momentum, grad in zip(old, new)]
        for old, new in zip(momenta, layer_grads)
    ]
    matrix = (1.0 + muon_mu) * factor * rows_grad.astype(jnp.float32)
    matrix = matrix + muon_mu * muon_mu * rows_momentum.astype(jnp.float32)
    gram = gram_sum(mat_dot(matrix, matrix.T))
    polar = polar_factor(gram)
    ortho = mat_dot(polar, matrix).astype(low)
    ortho = ortho.reshape(2, group, row_count, mp_count, piece_cols).transpose(0, 3, 1, 2, 4)
    ortho = ortho.reshape(dp_count * mp_count, row_count, piece_cols)
    back = lax.all_to_all(ortho, MATS, split_axis=0, concat_axis=0, tiled=True)
    back = back.reshape(4 * LAYERS, group, row_count, piece_cols)

    def joined(slot, width):
        pieces = back[slot][:, :, : width // group].transpose(1, 0, 2)
        return pieces.reshape(row_count, width).astype(jnp.float32)

    down_scale = math.sqrt(max(1.0, FF / D))
    ortho_layers = [
        (
            joined(4 * layer_index, up_proj.shape[2]),
            down_scale * joined(4 * layer_index + 1, up_proj.shape[2]),
            jnp.concatenate(
                [
                    joined(4 * layer_index + 2, width_qkv),
                    joined(4 * layer_index + 3, width_out),
                ],
                axis=1,
            ),
        )
        for layer_index in range(LAYERS)
    ]
    keep_factor = 1.0 - muon_rate * muon_decay
    updated = [
        weight * keep_factor - muon_rate * push
        for weight, push in zip((qkv_proj, out_proj, up_proj, down_proj), restored(ortho_layers))
    ]
    momenta_out = restored(momenta_new)
    return (
        loss,
        grad_norm,
        updated[0],
        momenta_out[0],
        updated[1],
        momenta_out[1],
        updated[2],
        momenta_out[2],
        updated[3],
        momenta_out[3],
        tables_updated,
        tables_first_new,
        tables_second_new,
        time_updated,
        time_first_new,
        time_second_new,
        mod_updated,
        mod_first_new,
        mod_second_new,
    )


def gram_sum(partial):
    half = partial.shape[0] // 2
    mine = lax.axis_index("pr")
    sent = lax.dynamic_slice_in_dim(partial, (1 - mine) * half, half, 0)
    kept = lax.dynamic_slice_in_dim(partial, mine * half, half, 0)
    kept = kept + swap(sent, ("pr", 0))
    kept = exchange_sum(kept, axis_bits("dm"))
    other_half = swap(kept, ("pr", 0))
    upper = mine == 1
    return jnp.concatenate(
        [jnp.where(upper, other_half, kept), jnp.where(upper, kept, other_half)], axis=0
    )


def solution(mesh):
    shape = mesh.devices.shape
    split = Mesh(mesh.devices.reshape(2, shape[0] // 4, 2, shape[1]), ALL)
    return jax.shard_map(
        body,
        mesh=split,
        in_specs=(
            P(DP, None, None),
            P(DP, None, None),
            P(DP),
            P(DP),
            P(None, DP),
            P(DP, None),
            P(DP, "mp"),
            P(None, DP, None, "mp"),
            P(None, "mp", DP),
            P(None, DP, "mp"),
            P(None, "mp", DP),
            P(None, DP, None, "mp"),
            P(None, "mp", DP),
            P(None, DP, "mp"),
            P(None, "mp", DP),
            P(None, DP),
            P(None, DP),
            P(DP, None),
            P(DP, None),
            P(DP, "mp"),
            P(DP, "mp"),
            P(),
        ),
        out_specs=(
            P(),
            P(),
            P(None, DP, None, "mp"),
            P(None, DP, None, "mp"),
            P(None, "mp", DP),
            P(None, "mp", DP),
            P(None, DP, "mp"),
            P(None, DP, "mp"),
            P(None, "mp", DP),
            P(None, "mp", DP),
            P(None, DP),
            P(None, DP),
            P(None, DP),
            P(DP, None),
            P(DP, None),
            P(DP, None),
            P(DP, "mp"),
            P(DP, "mp"),
            P(DP, "mp"),
        ),
        check_vma=False,
    )
```
